32 devices in a mesh: groups: 2 (over x), tile: 16 (over z, y, core).
Axes of the slice: x: 2, y: 2, z: 4, core: 2. Of those that a mesh axis runs over, the one named last changes fastest.
Arguments:
- hidden: bfloat16 [12288, 1152], P(('groups', 'tile')), parts along dimension 0, may hold values from -40 to 40
- keep_mask: int32 [12288], P(('groups', 'tile')), parts along dimension 0, may hold values 0 or 1
- kept_embed: bfloat16 [1152], replicated, may hold values from -6 to 6
- time_mod: bfloat16 [50, 6, 1152], replicated, may hold values from -3 to 3
- timestep: int32 [2], P('groups'), parts along dimension 0, may hold values from 0 to 49
- qkv_weight: bfloat16 [1152, 3456], replicated, may hold values from -0.1875 to 0.1875
- proj_weight: bfloat16 [1152, 1152], replicated, may hold values from -0.1875 to 0.1875
- norm_gain: bfloat16 [1152], replicated, may hold values from 0.099609375 to 1.8984375
- in_weight: bfloat16 [1152, 5760], P('tile'), may hold values from -0.1875 to 0.1875
- in_bias: bfloat16 [5760], replicated, may hold values from -3 to 3
- conv_weight: bfloat16 [3, 3, 5760], replicated, may hold values from -2 to 2
- conv_bias: bfloat16 [5760], replicated, may hold values from -3 to 3
- out_weight: bfloat16 [2880, 1152], P(None, 'tile'), may hold values from -0.109375 to 0.109375
Outputs:
- output: bfloat16 [12288, 1152], P(('groups', 'tile')), parts along dimension 0
The draws below stay inside these ranges and needn't reach their ends.
There are 2 independent parts, one for each index of `groups`. The reference program is written for one: setup_inputs(seed, part) draws one part's arguments, and reference() takes and returns one part's arrays. A program takes and returns all parts, laid end to end along the dimension named above; an argument that names none is the same for every part. Nothing has to cross between parts.
All inputs are finite; a program needn't handle non-finite values. No bound on the sum of `keep_mask` on one device may be relied on, other than what follows from the above.
Results may differ from the reference program's by a relative error of at most 0.0015.
The reference program's roundings to bfloat16 on the way (of `normed_in`, `normed_attn`, `normed_ffn`, `expanded` and `gated`) count: a program that leaves them out, or rounds other values in their place, can miss the bound.
Values may be sent and summed in bfloat16 or wider, within the bound.
A program may use at most 192 MiB of HBM per device.

```python
import math
import jax
import jax.numpy as jnp
from jax import lax

D = 1152
HEADS = 36
HEAD_DIM = 32
FF = 2880
CANVAS_W = 128
NSTEPS = 50
TOKENS = 6144


def draw_hidden(key, part):
    key_base, key_row, key_col = jax.random.split(key, 3)
    row_scale = jnp.exp(jax.random.uniform(key_row, (TOKENS, 1), jnp.float32, math.log(0.4), math.log(4.0)))
    col_scale = jnp.exp(jax.random.uniform(key_col, (1, D), jnp.float32, math.log(0.5), math.log(5.0)))
    base = jnp.clip(jax.random.normal(key_base, (TOKENS, D), jnp.float32), -3.0, 3.0)
    return jnp.clip(base * row_scale * col_scale, -40.0, 40.0).astype(jnp.bfloat16)


def place_ends(values, own_key, smallest, top_value):
    extent = values.shape
    spot = [jax.random.randint(jax.random.fold_in(own_key, axis), (), 0, extent[axis]) for axis in range(len(extent))]
    values = values.at[tuple(spot)].set(smallest)
    longest = extent.index(max(extent))
    spot[longest] = (spot[longest] + 1) % extent[longest]
    return values.at[tuple(spot)].set(top_value)


def levels(key, extent, shards, least, top_value):
    def one(axis_at, blocks):
        steps = jax.random.uniform(jax.random.fold_in(jax.random.fold_in(key, 6), axis_at), (blocks,), jnp.float32, least / len(shards), top_value / len(shards))
        return jnp.repeat(jnp.exp(steps), extent[axis_at] // blocks).reshape((-1,) + (1,) * (len(extent) - axis_at - 1))

    factor_of = one(*shards[0])
    for cut in shards[1:]:
        factor_of = factor_of * one(*cut)
    return factor_of


def scatter_about(own_key, extent, deviation, most, pieces=(), held_as=jnp.bfloat16):
    array = deviation * jax.random.normal(own_key, extent, jnp.float32)
    if pieces:
        array = array * levels(own_key, extent, pieces, -0.22, 0.18)
    return jnp.clip(array, -most, most).astype(held_as)


def setup_inputs(seed: int = 0, part: int = 0) -> dict:
    seeds = jax.random.split(jax.random.key(seed), 14)
    own_keys = jax.random.split(jax.random.fold_in(seeds[13], part), 14)
    hidden = draw_hidden(jax.random.fold_in(jax.random.fold_in(seeds[13], part), 71), part)
    keep_mask = place_ends((jax.random.randint(own_keys[1], (TOKENS,), 0, 2) < 1).astype(jnp.int32), jax.random.fold_in(own_keys[1], 1), 0, 1)
    kept_embed = scatter_about(seeds[2], (D,), 1.0, 6.0)
    time_mod = scatter_about(seeds[3], (NSTEPS, 6, D), 0.5, 3.0)
    timestep = jax.random.randint(own_keys[4], (1,), 0, NSTEPS).astype(jnp.int32)
    qkv_weight = scatter_about(seeds[5], (D, 3 * D), D ** -0.5, 0.1875)
    proj_weight = scatter_about(seeds[6], (D, D), D ** -0.5, 0.1875)
    norm_gain = jnp.clip(1.0 + 0.18 * jax.random.normal(seeds[7], (D,), jnp.float32), 0.099609375, 1.8984375).astype(jnp.bfloat16)
    in_weight = scatter_about(seeds[8], (D, 2 * FF), D ** -0.5, 0.1875, ((0, 16),))
    in_bias = scatter_about(seeds[9], (2 * FF,), 0.5, 3.0)
    conv_weight = scatter_about(seeds[10], (3, 3, 2 * FF), 9 ** -0.5, 2.0)
    conv_bias = scatter_about(seeds[11], (2 * FF,), 0.5, 3.0)
    out_weight = scatter_about(seeds[12], (FF, D), FF ** -0.5, 0.109375, ((1, 16),))
    return dict(hidden=hidden, keep_mask=keep_mask, kept_embed=kept_embed, time_mod=time_mod, timestep=timestep, qkv_weight=qkv_weight, proj_weight=proj_weight, norm_gain=norm_gain, in_weight=in_weight, in_bias=in_bias, conv_weight=conv_weight, conv_bias=conv_bias, out_weight=out_weight)


def modulated_norm(stream, shift, scale):
    factor = lax.rsqrt(lax.optimization_barrier(jnp.mean(stream * stream, axis=-1, keepdims=True)) + 1e-06)
    return stream * factor * (1.0 + scale) + shift

def convolve(window, conv_weight, conv_bias, count):
    width = window.shape[1] - 2
    total = jnp.zeros((count, width, window.shape[2]), jnp.float32) + conv_bias.astype(jnp.float32)
    for row_off in range(3):
        for col_off in range(3):
            total = total + window[row_off:row_off + count, col_off:col_off + width, :].astype(jnp.float32) * conv_weight[row_off, col_off].astype(jnp.float32)
    return total

def reference(hidden, keep_mask, kept_embed, time_mod, timestep, qkv_weight, proj_weight, norm_gain, in_weight, in_bias, conv_weight, conv_bias, out_weight):
    modulation = lax.dynamic_index_in_dim(time_mod, timestep[0], 0, keepdims=False).astype(jnp.float32)
    height = TOKENS // CANVAS_W
    blocks = height // 8
    span = 8 * CANVAS_W
    hidden_blocks = hidden.reshape(blocks, span, D)
    mask_blocks = keep_mask.reshape(blocks, span)
    embed = kept_embed.astype(jnp.float32)

    def residual_in(hidden_rows, mask_rows):
        return hidden_rows.astype(jnp.float32) + mask_rows.astype(jnp.float32)[:, None] * embed[None, :]

    def project(pair):
        stream = residual_in(pair[0], pair[1])
        normed_in = modulated_norm(stream, modulation[0], modulation[1]).astype(jnp.bfloat16)
        mixed_qkv = jnp.dot(normed_in, qkv_weight, preferred_element_type=jnp.float32)
        query = jax.nn.relu(mixed_qkv[:, :D]).astype(jnp.bfloat16)
        key_rows = jax.nn.relu(mixed_qkv[:, D:2 * D]).astype(jnp.bfloat16).reshape(span, HEADS, HEAD_DIM)
        values = mixed_qkv[:, 2 * D:].astype(jnp.bfloat16).reshape(span, HEADS, HEAD_DIM)
        partial_state = jnp.einsum('thd,the->hde', key_rows.astype(jnp.float32), values.astype(jnp.float32), precision=lax.Precision.HIGHEST)
        return (query, partial_state)
    queries, partials = lax.map(project, (hidden_blocks, mask_blocks))
    state = lax.optimization_barrier(jnp.sum(partials, axis=0))

    def attend(triple):
        stream = residual_in(triple[0], triple[1])
        query = triple[2].reshape(span, HEADS, HEAD_DIM).astype(jnp.float32)
        attended = jnp.einsum('thd,hde->the', query, state, precision=lax.Precision.HIGHEST).reshape(span, D)
        factor = lax.rsqrt(lax.optimization_barrier(jnp.mean(attended * attended, axis=-1, keepdims=True)) + 1e-06)
        normed_attn = (attended * factor * norm_gain.astype(jnp.float32)).astype(jnp.bfloat16)
        after_attn = stream + modulation[2] * jnp.dot(normed_attn, proj_weight, preferred_element_type=jnp.float32)
        normed_ffn = modulated_norm(after_attn, modulation[3], modulation[4]).astype(jnp.bfloat16)
        expanded = jax.nn.silu(jnp.dot(normed_ffn, in_weight, preferred_element_type=jnp.float32) + in_bias.astype(jnp.float32)).astype(jnp.bfloat16)
        return (after_attn, expanded)
    residuals, expanded = lax.map(attend, (hidden_blocks, mask_blocks, queries))
    grid = expanded.reshape(height, CANVAS_W, 2 * FF)
    padded = jnp.pad(grid, ((1, 1), (1, 1), (0, 0)))

    def finish(pair):
        first = pair[0] * 8
        window = lax.dynamic_slice_in_dim(padded, first, 10, 0)
        conv = convolve(window, conv_weight, conv_bias, 8)
        gated = (conv[..., :FF] * jax.nn.silu(conv[..., FF:])).astype(jnp.bfloat16).reshape(span, FF)
        return (pair[1] + modulation[5] * jnp.dot(gated, out_weight, preferred_element_type=jnp.float32)).astype(jnp.bfloat16)
    result = lax.map(finish, (jnp.arange(blocks, dtype=jnp.int32), residuals))
    return result.reshape(TOKENS, D)
```

```python
import functools

import jax
import jax.numpy as jnp
from jax import lax
from jax.experimental import pallas as pl
from jax.experimental.pallas import tpu as pltpu
from jax.sharding import PartitionSpec as P

D = 1152
HEADS = 36
HEAD_DIM = 32
FF = 2880
CANVAS_W = 128
LANES = 128
PACK = LANES // HEAD_DIM
GROUPS = D // LANES
MESH = pl.DeviceIdType.MESH


def mesh_box(n):
    wide = 1
    while (2 * wide) ** 2 <= n // 2:
        wide *= 2
    return n // (2 * wide), wide


STEPS = -(-FF // LANES)
SPLIT = FF % LANES
AHEAD = 3
LAG_SIDE = 2
LAG_PLANE = 4
LAG_USE = 5
LAG_SENT = 8


def repeat(lo, hi, do):
    if hi - lo <= 4:
        for k in range(lo, hi):
            do(k)
        return

    def body(k, _):
        do(k)
        return 0

    lax.fori_loop(lo, hi, body, 0)


def modulated_norm(stream, shift, scale):
    factor = lax.rsqrt(jnp.mean(stream * stream, axis=-1, keepdims=True) + 1e-06)
    return stream * factor * (1.0 + scale) + shift


def silu(v):
    half = 0.5 * v
    return half * (1.0 + jnp.tanh(half))


def kernel(
    n,
    hidden_ref,
    mask_ref,
    embed_ref,
    mod_ref,
    qkv_hbm,
    proj_hbm,
    gain_ref,
    in_ref,
    outw_ref,
    table_ref,
    out_ref,
    qkv_ref,
    proj_ref,
    after_ref,
    frame_ref,
    mixed,
    part,
    landed,
    mine,
    state,
    normed,
    acc_ref,
    wide,
    wide32,
    land,
    send1,
    recv1,
    send2,
    recv2,
    halo_send,
    halo_recv,
    line_send,
    line_recv,
    side_send,
    side_recv,
    far_send,
    far_recv,
    plane_send,
    plane_recv,
    twin_send,
    twin_recv,
    load_sem,
    own_sem,
):
    count_a, count_b = mesh_box(n)
    me = lax.axis_index("tile")
    plane = lax.axis_index("groups")
    core = lax.rem(me, 2)
    at_b = lax.rem(me // 2, count_b)
    at_a = me // (2 * count_b)
    rows = in_ref.shape[0]
    per = mine.shape[0]
    tokens = hidden_ref.shape[0]

    def tile_of(a, b, c):
        return (a * count_b + b) * 2 + c

    loads = [
        pltpu.make_async_copy(
            qkv_hbm.at[:, j * D : (j + 1) * D], qkv_ref.at[j % 2], load_sem.at[j]
        )
        for j in range(3)
    ]
    loads.append(pltpu.make_async_copy(proj_hbm, proj_ref, load_sem.at[3]))
    for j in (0, 1, 3):
        loads[j].start()

    barrier = pltpu.get_barrier_semaphore()

    def greet(k, _):
        pl.semaphore_signal(
            barrier, inc=1, device_id={"tile": lax.rem(me + k, n)}, device_id_type=MESH
        )
        return 0

    lax.fori_loop(1, n, greet, 0)
    pl.semaphore_signal(barrier, inc=1, device_id={"groups": 1 - plane}, device_id_type=MESH)
    pl.semaphore_wait(barrier, n)

    def remote(ref, send, recv, target):
        return pltpu.make_async_remote_copy(
            src_ref=ref,
            dst_ref=ref,
            send_sem=send,
            recv_sem=recv,
            device_id=target,
            device_id_type=MESH,
        )

    def active(q):
        return lax.rem(plane + q, 2) == 0

    def other(k):
        return lax.rem(at_a + k, count_a)

    def beside(k):
        return lax.rem(at_b + k, count_b)

    def near(a):
        return jnp.abs(a - at_a) == 1

    def line(q, a):
        ref = land.at[q, at_a, at_b, core]
        to = {"tile": tile_of(a, at_b, core)}
        return remote(ref, line_send.at[q, a], line_recv.at[q, at_a], to)

    def line_in(q, a):
        ref = land.at[q, a, at_b, core]
        to = {"tile": tile_of(a, at_b, core)}
        return remote(ref, own_sem, line_recv.at[q, a], to)

    def side(q, b, whole):
        ref = land.at[q, :, at_b, core] if whole else land.at[q, at_a, at_b, core]
        to = {"tile": tile_of(at_a, b, core)}
        return remote(ref, side_send.at[q, b], side_recv.at[q, at_b], to)

    def side_in(q, b, whole):
        ref = land.at[q, :, b, core] if whole else land.at[q, at_a, b, core]
        to = {"tile": tile_of(at_a, b, core)}
        return remote(ref, own_sem, side_recv.at[q, b], to)

    def far(q, a):
        ref = land.at[q, a, at_b, core]
        return remote(ref, far_send.at[q, a], far_recv.at[q, a], {"groups": 1 - plane})

    def across(q, a, b):
        ref = land.at[q, a, b, core]
        return remote(ref, plane_send.at[q], plane_recv.at[q], {"groups": 1 - plane})

    def across_all(q):
        ref = land.at[q, pl.ds(0, count_a - 1), pl.ds(0, count_b - 1), core]
        return remote(ref, plane_send.at[q], plane_recv.at[q], {"groups": 1 - plane})

    def twin(q):
        ref = land.at[q, :, :, core]
        to = {"tile": tile_of(at_a, at_b, 1 - core)}
        return remote(ref, twin_send.at[q], twin_recv.at[q], to)

    def twin_in(q):
        ref = land.at[q, :, :, 1 - core]
        to = {"tile": tile_of(at_a, at_b, 1 - core)}
        return remote(ref, own_sem, twin_recv.at[q], to)

    def build(q):
        first = pl.multiple_of(q * LANES, LANES)
        second = pl.multiple_of(q * LANES + FF - SPLIT, LANES)
        a = in_ref[:, pl.ds(first, LANES)]
        b = in_ref[:, pl.ds(second, 2 * LANES)][:, SPLIT : SPLIT + LANES]
        o = outw_ref[:, pl.ds(first, LANES)]
        land[q, at_a, at_b, core] = jnp.concatenate([a, b, o], axis=1)

    def build_last():
        q = STEPS - 1
        none = jnp.zeros((rows, LANES - SPLIT), jnp.bfloat16)
        a = in_ref[:, q * LANES : FF]
        b = in_ref[:, FF + q * LANES : 2 * FF]
        o = outw_ref[:, q * LANES : FF]
        land[q, at_a, at_b, core] = jnp.concatenate([a, none, b, none, o, none], axis=1)

    def gated(q, do):
        if isinstance(q, int):
            if 0 <= q < STEPS:
                do(q)
        else:
            pl.when(jnp.logical_and(q >= 0, q < STEPS))(lambda: do(q))

    def start_own(q):
        if isinstance(q, int):
            build(q) if q < STEPS - 1 else build_last()
        else:
            pl.when(q < STEPS - 1)(lambda: build(q))
            pl.when(q == STEPS - 1)(build_last)

        def one(k):
            a = other(k)

            @pl.when(jnp.logical_or(near(a), active(q)))
            def _():
                line(q, a).start()

        repeat(1, count_a, one)

        @pl.when(jnp.logical_not(active(q)))
        def _():
            repeat(1, count_b, lambda k: side(q, beside(k), False).start())

    def pass_lines(q):
        @pl.when(active(q))
        def _():
            repeat(1, count_a, lambda k: line_in(q, other(k)).wait_recv())
            repeat(1, count_b, lambda k: side(q, beside(k), True).start())

            def one(k):
                a = other(k)

                @pl.when(jnp.logical_not(near(a)))
                def _():
                    far(q, a).start()

            repeat(1, count_a, one)

    def pass_sides(q):
        @pl.when(active(q))
        def _():
            def one(k):
                b = beside(k)
                side_in(q, b, True).wait_recv()
                repeat(1, count_a, lambda m: across(q, other(m), b).start())

            repeat(1, count_b, one)
            twin(q).start()

    def pass_planes(q):
        @pl.when(jnp.logical_not(active(q)))
        def _():
            def one(k):
                a = other(k)

                @pl.when(near(a))
                def _():
                    line_in(q, a).wait_recv()

                @pl.when(jnp.logical_not(near(a)))
                def _():
                    far(q, a).wait_recv()

            repeat(1, count_a, one)
            repeat(1, count_b, lambda k: side_in(q, beside(k), False).wait_recv())
            across_all(q).wait_recv()
            twin(q).start()

    def settle(q):
        def one(k):
            a = other(k)

            @pl.when(jnp.logical_or(near(a), active(q)))
            def _():
                line(q, a).wait_send()

            @pl.when(jnp.logical_and(jnp.logical_not(near(a)), active(q)))
            def _():
                far(q, a).wait_send()

        repeat(1, count_a, one)

        @pl.when(active(q))
        def _():
            repeat(1, count_b, lambda k: side(q, beside(k), True).wait_send())
            across_all(q).wait_send()

        @pl.when(jnp.logical_not(active(q)))
        def _():
            repeat(1, count_b, lambda k: side(q, beside(k), False).wait_send())

        twin(q).wait_send()

    def slot(s):
        gated(s + AHEAD, start_own)
        gated(s, pass_lines)
        gated(s - LAG_SIDE, pass_sides)
        gated(s - LAG_PLANE, pass_planes)
        gated(s - LAG_SENT, settle)

    for q in range(AHEAD):
        start_own(q)

    stream = hidden_ref[...].astype(jnp.float32) + mask_ref[...] * embed_ref[...]
    normed[...] = modulated_norm(stream, mod_ref[0:1, :], mod_ref[1:2, :]).astype(jnp.bfloat16)
    after_ref[...] = stream
    span = D // 3

    def project(third):
        def body(i, _):
            cols = pl.ds(pl.multiple_of(i * span, LANES), span)
            out = jnp.dot(
                normed[...], qkv_ref[third % 2, :, cols], preferred_element_type=jnp.float32
            )
            if third < 2:
                out = jnp.maximum(out, 0.0)
            to = pl.ds(pl.multiple_of(third * D + i * span, LANES), span)
            mixed[:, to] = out.astype(jnp.bfloat16)
            return 0

        loads[third].wait()
        lax.fori_loop(0, 3, body, 0)
        if third == 0:
            loads[2].start()
        slot(third)

    for third in range(3):
        project(third)
    row_head = lax.broadcasted_iota(jnp.int32, (LANES, LANES), 0) // HEAD_DIM
    col_head = lax.broadcasted_iota(jnp.int32, (LANES, LANES), 1) // HEAD_DIM
    same = row_head == col_head
    part[...] = jnp.zeros_like(part)

    def outer(g, _):
        first = pl.multiple_of(g * LANES, LANES)
        product = lax.dot_general(
            mixed[:, pl.ds(D + first, LANES)],
            mixed[:, pl.ds(2 * D + first, LANES)],
            (((0,), (0,)), ((), ())),
            preferred_element_type=jnp.float32,
        )
        product = jnp.where(same, product, 0.0)
        packed = product[:HEAD_DIM]
        for h in range(1, PACK):
            packed = packed + product[h * HEAD_DIM : (h + 1) * HEAD_DIM]
        part[pl.ds(pl.multiple_of(g * HEAD_DIM, HEAD_DIM), HEAD_DIM), :] = packed
        return 0

    lax.fori_loop(0, GROUPS, outer, 0)

    def piece(ref, k):
        return ref.at[pl.ds(pl.multiple_of(k * per, 8), per)]

    def scatter(k):
        peer = lax.rem(me + k, n)
        return pltpu.make_async_remote_copy(
            src_ref=piece(part, peer),
            dst_ref=landed.at[k],
            send_sem=send1.at[k],
            recv_sem=recv1.at[k],
            device_id={"tile": peer},
            device_id_type=MESH,
        )

    def share(k):
        return pltpu.make_async_remote_copy(
            src_ref=mine,
            dst_ref=piece(state, me),
            send_sem=send2.at[k],
            recv_sem=recv2.at[k],
            device_id={"tile": lax.rem(me + k, n)},
            device_id_type=MESH,
        )

    def each(do):
        def body(k, _):
            do(k)
            return 0

        lax.fori_loop(1, n, body, 0)

    each(lambda k: scatter(k).start())
    slot(3)
    mine[...] = part[pl.ds(pl.multiple_of(me * per, 8), per), :]

    def gather(k):
        scatter(k).wait_recv()
        mine[...] += landed[k]

    each(gather)
    each(lambda k: share(k).start())
    state[pl.ds(pl.multiple_of(me * per, 8), per), :] = mine[...]
    slot(4)
    each(lambda k: scatter(k).wait_send())
    each(lambda k: share(k).wait())

    pieces = []
    for g in range(GROUPS):
        block = jnp.concatenate([state[g * HEAD_DIM : (g + 1) * HEAD_DIM, :]] * PACK, axis=0)
        block = jnp.where(same, block, 0.0)
        pieces.append(
            jnp.dot(
                mixed[:, g * LANES : (g + 1) * LANES].astype(jnp.float32),
                block,
                precision=lax.Precision.HIGHEST,
                preferred_element_type=jnp.float32,
            )
        )
    attended = jnp.concatenate(pieces, axis=1)
    factor = lax.rsqrt(jnp.mean(attended * attended, axis=-1, keepdims=True) + 1e-06)
    normed[...] = (attended * factor * gain_ref[...]).astype(jnp.bfloat16)
    slot(5)
    loads[3].wait()

    def attach(j, _):
        cols = pl.ds(pl.multiple_of(j * span, LANES), span)
        out = jnp.dot(normed[...], proj_ref[:, cols], preferred_element_type=jnp.float32)
        after_ref[:, cols] += mod_ref[2:3, cols] * out
        return 0

    lax.fori_loop(0, 3, attach, 0)
    frame_ref[CANVAS_W : CANVAS_W + tokens, :] = modulated_norm(
        after_ref[...], mod_ref[3:4, :], mod_ref[4:5, :]
    ).astype(jnp.bfloat16)

    def halo(way):
        lo = tokens if way == 0 else CANVAS_W
        to = 0 if way == 0 else CANVAS_W + tokens
        return pltpu.make_async_remote_copy(
            src_ref=frame_ref.at[lo : lo + CANVAS_W],
            dst_ref=frame_ref.at[to : to + CANVAS_W],
            send_sem=halo_send.at[way],
            recv_sem=halo_recv.at[way],
            device_id={"tile": me + (1 if way == 0 else -1)},
            device_id_type=MESH,
        )

    has = (me < n - 1, me > 0)
    for way in range(2):
        @pl.when(has[way])
        def _():
            halo(way).start()

    @pl.when(me == 0)
    def _():
        frame_ref[:CANVAS_W, :] = jnp.zeros((CANVAS_W, D), jnp.bfloat16)

    @pl.when(me == n - 1)
    def _():
        frame_ref[CANVAS_W + tokens :, :] = jnp.zeros((CANVAS_W, D), jnp.bfloat16)

    slot(6)
    slot(7)
    for way in range(2):
        @pl.when(has[way])
        def _():
            halo(way).wait_send()

        @pl.when(has[1 - way])
        def _():
            halo(way).wait_recv()

    frame = frame_ref.shape[0]
    edge = [jnp.where(has[1 - way], 1.0, 0.0).astype(jnp.float32) for way in range(2)]
    column = lax.broadcasted_iota(jnp.int32, (CANVAS_W, 2 * LANES), 0)
    not_left = column > 0
    not_right = column < CANVAS_W - 1
    acc_ref[...] = jnp.zeros_like(acc_ref)

    def use(q):
        twin_in(q).wait_recv()
        for j in range(3 if rows % 8 else 1):
            for t in range(n):
                a, b, c = t // (2 * count_b), t // 2 % count_b, t % 2
                if rows % 8 == 0:
                    wide[t * rows : (t + 1) * rows, :] = land[q, a, b, c]
                else:
                    block = land[q, a, b, c, :, j * LANES : (j + 1) * LANES]
                    wide32[t * rows : (t + 1) * rows, :] = block.astype(jnp.float32)
            if rows % 8:
                wide[:, j * LANES : (j + 1) * LANES] = wide32[...].astype(jnp.bfloat16)
        p = table_ref[q]
        v = jnp.dot(frame_ref[...], wide[:, : 2 * LANES], preferred_element_type=jnp.float32)
        e = silu(v + p[10:11, :]).astype(jnp.bfloat16).astype(jnp.float32)
        lines = [e[r * CANVAS_W : (r + 1) * CANVAS_W] for r in range(frame // CANVAS_W)]
        lines[0] = lines[0] * edge[0]
        lines[-1] = lines[-1] * edge[1]
        out = []
        for r in range(tokens // CANVAS_W):
            way = []
            for j in range(3):
                way.append(
                    lines[r] * p[j : j + 1, :]
                    + lines[r + 1] * p[3 + j : 4 + j, :]
                    + lines[r + 2] * p[6 + j : 7 + j, :]
                )
            left = jnp.where(not_left, pltpu.roll(way[0], 1, 0), 0.0)
            right = jnp.where(not_right, pltpu.roll(way[2], CANVAS_W - 1, 0), 0.0)
            conv = left + way[1] + right + p[9:10, :]
            out.append((conv[:, :LANES] * silu(conv[:, LANES:])).astype(jnp.bfloat16))
        acc_ref[...] += lax.dot_general(
            jnp.concatenate(out, axis=0),
            wide[:, 2 * LANES :],
            (((1,), (1,)), ((), ())),
            preferred_element_type=jnp.float32,
        )

    begin = 8
    double = 0
    while 2 * double + 1 <= begin + double - LAG_USE:
        double += 1

    def catch_up(i, _):
        slot(begin + i)
        use(2 * i)
        use(2 * i + 1)
        return 0

    lax.fori_loop(0, double, catch_up, 0)
    shift = begin + double - 2 * double

    def follow(q, _):
        slot(q + shift)
        use(q)
        return 0

    lax.fori_loop(2 * double, STEPS, follow, 0)
    out_ref[...] = (after_ref[...] + mod_ref[5:6, :] * acc_ref[...]).astype(out_ref.dtype)

    def finish(q, _):
        settle(q)
        return 0

    lax.fori_loop(STEPS - 1 + shift - LAG_SENT + 1, STEPS, finish, 0)


def block(hidden, mask, embed, mod, qkv_weight, proj_weight, gain, in_weight, out_weight, table, n):
    count_a, count_b = mesh_box(n)
    rows = in_weight.shape[0]
    tokens = hidden.shape[0]
    per = -(-GROUPS * HEAD_DIM // (8 * n)) * 8
    vmem = pl.BlockSpec(memory_space=pltpu.VMEM)
    hbm = pl.BlockSpec(memory_space=pl.ANY)
    dma = pltpu.SemaphoreType.DMA
    bf16 = jnp.bfloat16
    return pl.pallas_call(
        functools.partial(kernel, n),
        out_shape=jax.ShapeDtypeStruct((tokens, D), bf16),
        in_specs=[vmem] * 4 + [hbm] * 2 + [vmem] * 4,
        out_specs=vmem,
        scratch_shapes=[
            pltpu.VMEM((2, D, D), bf16),
            pltpu.VMEM((D, D), bf16),
            pltpu.VMEM((tokens, D), jnp.float32),
            pltpu.VMEM((tokens + 2 * CANVAS_W, D), bf16),
            pltpu.VMEM((tokens, 3 * D), bf16),
            pltpu.VMEM((n * per, LANES), jnp.float32),
            pltpu.VMEM((n, per, LANES), jnp.float32),
            pltpu.VMEM((per, LANES), jnp.float32),
            pltpu.VMEM((n * per, LANES), jnp.float32),
            pltpu.VMEM((tokens, D), bf16),
            pltpu.VMEM((tokens, D), jnp.float32),
            pltpu.VMEM((D, 3 * LANES), bf16),
            pltpu.VMEM((D if rows % 8 else 8, LANES), jnp.float32),
            pltpu.VMEM((STEPS, count_a, count_b, 2, rows, 3 * LANES), bf16),
            dma((n,)),
            dma((n,)),
            dma((n,)),
            dma((n,)),
            dma((2,)),
            dma((2,)),
            dma((STEPS, count_a)),
            dma((STEPS, count_a)),
            dma((STEPS, count_b)),
            dma((STEPS, count_b)),
            dma((STEPS, count_a)),
            dma((STEPS, count_a)),
            dma((STEPS,)),
            dma((STEPS,)),
            dma((STEPS,)),
            dma((STEPS,)),
            dma((4,)),
            dma,
        ],
        compiler_params=pltpu.CompilerParams(
            collective_id=0, has_side_effects=True, vmem_limit_bytes=60 << 20
        ),
    )(hidden, mask, embed, mod, qkv_weight, proj_weight, gain, in_weight, out_weight, table)


def local(
    n,
    hidden,
    keep_mask,
    kept_embed,
    time_mod,
    timestep,
    qkv_weight,
    proj_weight,
    norm_gain,
    in_weight,
    in_bias,
    conv_weight,
    conv_bias,
    out_weight,
):
    f32 = jnp.float32
    small = jnp.concatenate(
        [
            conv_weight.reshape(9, 2 * FF).astype(f32),
            conv_bias.astype(f32)[None],
            in_bias.astype(f32)[None],
            jnp.zeros((5, 2 * FF), f32),
        ],
        axis=0,
    )
    fill = ((0, 0), (0, STEPS * LANES - FF))
    table = jnp.stack(
        [jnp.pad(half, fill).reshape(16, STEPS, LANES) for half in (small[:, :FF], small[:, FF:])],
        axis=2,
    )
    table = table.transpose(1, 0, 2, 3).reshape(STEPS, 16, 2 * LANES)
    modulation = lax.dynamic_index_in_dim(time_mod, timestep[0], 0, keepdims=False).astype(f32)
    return block(
        hidden,
        keep_mask.astype(f32)[:, None],
        kept_embed.astype(f32)[None],
        modulation,
        qkv_weight,
        proj_weight,
        norm_gain.astype(f32)[None],
        in_weight,
        out_weight.T,
        table,
        n,
    )


def solution(mesh):
    in_specs = (
        P(("groups", "tile"), None),
        P(("groups", "tile")),
        P(),
        P(),
        P("groups"),
        P(),
        P(),
        P(),
        P("tile", None),
        P(),
        P(),
        P(),
        P(None, "tile"),
    )
    return jax.shard_map(
        functools.partial(local, mesh.shape["tile"]),
        mesh=mesh,
        in_specs=in_specs,
        out_specs=P(("groups", "tile"), None),
        check_vma=False,
    )
```

```python
import functools

import jax
import jax.numpy as jnp
from jax import lax
from jax.experimental import pallas as pl
from jax.experimental.pallas import tpu as pltpu
from jax.sharding import PartitionSpec as P

D = 1152
HEADS = 36
HEAD_DIM = 32
FF = 2880
CANVAS_W = 128
LANES = 128
PACK = LANES // HEAD_DIM
GROUPS = D // LANES
MESH = pl.DeviceIdType.MESH


def mesh_box(n):
    wide = 1
    while (2 * wide) ** 2 <= n // 2:
        wide *= 2
    return n // (2 * wide), wide


STEPS = -(-FF // LANES)
SPLIT = FF % LANES
PAIR = 2 * LANES
TEAMS = -(-STEPS // 2)
AHEAD = 2
LAG_SIDE = 1
LAG_PLANE = 2
LAG_USE = 3
SITES = (1, 3, 4, 5, 6, 7)
EARLY = len(SITES)


def width(g):
    return min(2, STEPS - 2 * g)


def repeat(lo, hi, do):
    if hi - lo <= 4:
        for k in range(lo, hi):
            do(k)
        return

    def body(k, _):
        do(k)
        return 0

    lax.fori_loop(lo, hi, body, 0)


def modulated_norm(stream, shift, scale):
    factor = lax.rsqrt(jnp.mean(stream * stream, axis=-1, keepdims=True) + 1e-06)
    return stream * factor * (1.0 + scale) + shift


def silu(v):
    half = 0.5 * v
    return half * (1.0 + jnp.tanh(half))


def kernel(
    n,
    step_ref,
    hidden_ref,
    mask_ref,
    embed_ref,
    time_ref,
    qkv_hbm,
    proj_hbm,
    gain_ref,
    in_ref,
    in_bias_ref,
    conv_ref,
    conv_bias_ref,
    outw_ref,
    out_ref,
    qkv_ref,
    proj_ref,
    after_ref,
    frame_ref,
    mixed,
    part,
    landed,
    mine,
    state,
    acc_ref,
    wide32,
    flat_ref,
    table_ref,
    mod_ref,
    land,
    send1,
    recv1,
    send2,
    recv2,
    halo_send,
    halo_recv,
    line_send,
    line_recv,
    side_send,
    side_recv,
    far_send,
    plane_send,
    twin_send,
    twin_recv,
    load_sem,
    own_sem,
):
    count_a, count_b = mesh_box(n)
    me = lax.axis_index("tile")
    plane = lax.axis_index("groups")
    core = lax.rem(me, 2)
    at_b = lax.rem(me // 2, count_b)
    at_a = me // (2 * count_b)
    rows = in_ref.shape[0]
    per = mine.shape[0]
    tokens = hidden_ref.shape[0]
    normed = frame_ref.at[CANVAS_W : CANVAS_W + tokens]
    wide = qkv_ref.at[0, :, : 6 * LANES]

    def tile_of(a, b, c):
        return (a * count_b + b) * 2 + c

    loads = [
        pltpu.make_async_copy(
            qkv_hbm.at[:, j * D : (j + 1) * D], qkv_ref.at[j % 2], load_sem.at[j]
        )
        for j in range(3)
    ]
    loads.append(pltpu.make_async_copy(proj_hbm, proj_ref, load_sem.at[3]))
    for j in (0, 1, 3):
        loads[j].start()

    barrier = pltpu.get_barrier_semaphore()

    def greet(k, _):
        pl.semaphore_signal(
            barrier, inc=1, device_id={"tile": lax.rem(me + k, n)}, device_id_type=MESH
        )
        return 0

    lax.fori_loop(1, n, greet, 0)
    pl.semaphore_signal(barrier, inc=1, device_id={"groups": 1 - plane}, device_id_type=MESH)
    pl.semaphore_wait(barrier, n)

    def remote(ref, send, recv, target):
        return pltpu.make_async_remote_copy(
            src_ref=ref,
            dst_ref=ref,
            send_sem=send,
            recv_sem=recv,
            device_id=target,
            device_id_type=MESH,
        )

    def active(q):
        return lax.rem(plane + q, 2) == 0

    def other(k):
        return lax.rem(at_a + k, count_a)

    def beside(k):
        return lax.rem(at_b + k, count_b)

    def near(a):
        return jnp.abs(a - at_a) == 1

    def span_of(g):
        return pl.ds(2 * g, width(g) if isinstance(g, int) else 2)

    def line(g, a):
        ref = land.at[span_of(g), at_a, at_b, core]
        to = {"tile": tile_of(a, at_b, core)}
        return remote(ref, line_send.at[a], line_recv.at[g], to)

    def side(g, b, whole):
        if whole:
            ref = land.at[span_of(g), :, at_b, core]
        else:
            ref = land.at[span_of(g), at_a, at_b, core]
        to = {"tile": tile_of(at_a, b, core)}
        return remote(ref, side_send.at[int(whole), b], side_recv.at[g], to)

    def far(g, a):
        ref = land.at[span_of(g), a, at_b, core]
        return remote(ref, far_send.at[a], line_recv.at[g], {"groups": 1 - plane})

    def across(g, a, b):
        ref = land.at[span_of(g), a, b, core]
        return remote(ref, plane_send, side_recv.at[g], {"groups": 1 - plane})

    def twin(g):
        ref = land.at[span_of(g), :, :, core]
        to = {"tile": tile_of(at_a, at_b, 1 - core)}
        return remote(ref, twin_send, twin_recv.at[g], to)

    def twin_in(g):
        ref = land.at[span_of(g), :, :, 1 - core]
        to = {"tile": tile_of(at_a, at_b, 1 - core)}
        return remote(ref, own_sem, twin_recv.at[g], to)

    def own_side_in(g):
        ref = land.at[span_of(g), pl.ds(0, count_a - 1), at_b, core]
        return remote(ref, own_sem, line_recv.at[g], {"groups": 1 - plane})

    def other_side_in(g):
        ref = land.at[span_of(g), :, pl.ds(0, count_b - 1), core]
        return remote(ref, own_sem, side_recv.at[g], {"groups": 1 - plane})

    def build(q):
        first = pl.multiple_of(q * LANES, LANES)
        second = pl.multiple_of(q * LANES + FF - SPLIT, LANES)
        a = in_ref[:, pl.ds(first, LANES)]
        b = in_ref[:, pl.ds(second, 2 * LANES)][:, SPLIT : SPLIT + LANES]
        o = outw_ref[:, pl.ds(first, LANES)]
        land[q, at_a, at_b, core] = jnp.concatenate([a, b, o], axis=1)

    def build_last():
        q = STEPS - 1
        none = jnp.zeros((rows, LANES - SPLIT), jnp.bfloat16)
        a = in_ref[:, q * LANES : FF]
        b = in_ref[:, FF + q * LANES : 2 * FF]
        o = outw_ref[:, q * LANES : FF]
        land[q, at_a, at_b, core] = jnp.concatenate([a, none, b, none, o, none], axis=1)

    def gated(g, do):
        if isinstance(g, int):
            if 0 <= g < TEAMS:
                do(g)
        else:
            pl.when(jnp.logical_and(g >= 0, g < TEAMS - 1))(lambda: do(g))
            pl.when(g == TEAMS - 1)(lambda: do(TEAMS - 1))

    def start_own(g):
        if isinstance(g, int):
            for q in range(2 * g, 2 * g + width(g)):
                build(q) if q < STEPS - 1 else build_last()
        else:
            build(2 * g)
            build(2 * g + 1)

        def one(k):
            a = other(k)

            @pl.when(jnp.logical_or(near(a), active(g)))
            def _():
                line(g, a).start()

        repeat(1, count_a, one)

        @pl.when(jnp.logical_not(active(g)))
        def _():
            repeat(1, count_b, lambda k: side(g, beside(k), False).start())

    def pass_lines(g):
        @pl.when(active(g))
        def _():
            own_side_in(g).wait_recv()
            repeat(1, count_b, lambda k: side(g, beside(k), True).start())

            def one(k):
                a = other(k)

                @pl.when(jnp.logical_not(near(a)))
                def _():
                    far(g, a).start()

            repeat(1, count_a, one)

    def pass_sides(g):
        @pl.when(active(g))
        def _():
            other_side_in(g).wait_recv()

            def one(k):
                b = beside(k)
                repeat(1, count_a, lambda m: across(g, other(m), b).start())

            repeat(1, count_b, one)
            twin(g).start()

    def pass_planes(g):
        @pl.when(jnp.logical_not(active(g)))
        def _():
            own_side_in(g).wait_recv()
            other_side_in(g).wait_recv()
            twin(g).start()

    def sent(ref, sem):
        remote(ref, sem, line_recv.at[0], {"groups": 1 - plane}).wait_send()

    def settle():
        shares = [sum(width(g) for g in range(TEAMS) if g % 2 == p) for p in range(2)]

        def one(k):
            a = other(k)
            pl.when(near(a))(lambda: sent(land.at[:, at_a, at_b, core], line_send.at[a]))
            for p in range(2):
                @pl.when(jnp.logical_and(jnp.logical_not(near(a)), plane == p))
                def _():
                    some = land.at[pl.ds(0, shares[p]), at_a, at_b, core]
                    sent(some, line_send.at[a])
                    sent(some, far_send.at[a])

        repeat(1, count_a, one)
        for p in range(2):
            @pl.when(plane == p)
            def _():
                on, off = pl.ds(0, shares[p]), pl.ds(0, shares[1 - p])

                def two(k):
                    b = beside(k)
                    sent(land.at[on, :, at_b, core], side_send.at[1, b])
                    sent(land.at[off, at_a, at_b, core], side_send.at[0, b])

                repeat(1, count_b, two)
                most = pl.ds(0, count_a - 1)
                sent(land.at[on, most, pl.ds(0, count_b - 1), core], plane_send)

        sent(land.at[:, :, :, core], twin_send)

    def slot(s):
        gated(s + AHEAD, start_own)
        gated(s, pass_lines)
        gated(s - LAG_SIDE, pass_sides)
        gated(s - LAG_PLANE, pass_planes)

    def tick(site):
        for s, where in enumerate(SITES):
            if where == site:
                slot(s)

    for g in range(AHEAD):
        start_own(g)

    step_at = lax.broadcasted_iota(jnp.int32, time_ref.shape[1:], 0) == step_ref[0]
    for j in range(6):
        picked = jnp.where(step_at, time_ref[j].astype(jnp.float32), 0.0)
        mod_ref[j : j + 1, :] = jnp.sum(picked, axis=0, keepdims=True)
    mask = mask_ref[...].astype(jnp.float32).reshape(tokens, 1)
    embed = embed_ref[...].astype(jnp.float32).reshape(1, D)
    stream = hidden_ref[...].astype(jnp.float32) + mask * embed
    normed[...] = modulated_norm(stream, mod_ref[0:1, :], mod_ref[1:2, :]).astype(jnp.bfloat16)
    after_ref[...] = stream
    span = D // 3

    def project(third):
        def body(i, _):
            cols = pl.ds(pl.multiple_of(i * span, LANES), span)
            out = jnp.dot(
                normed[...], qkv_ref[third % 2, :, cols], preferred_element_type=jnp.float32
            )
            if third < 2:
                out = jnp.maximum(out, 0.0)
            to = pl.ds(pl.multiple_of(third * D + i * span, LANES), span)
            mixed[:, to] = out.astype(jnp.bfloat16)
            return 0

        loads[third].wait()
        lax.fori_loop(0, 3, body, 0)
        if third == 0:
            loads[2].start()
        tick(1 + third)

    tick(0)
    for third in range(3):
        project(third)
    row_head = lax.broadcasted_iota(jnp.int32, (LANES, LANES), 0) // HEAD_DIM
    col_head = lax.broadcasted_iota(jnp.int32, (LANES, LANES), 1) // HEAD_DIM
    same = row_head == col_head
    part[...] = jnp.zeros_like(part)

    def outer(g, _):
        first = pl.multiple_of(g * LANES, LANES)
        product = lax.dot_general(
            mixed[:, pl.ds(D + first, LANES)],
            mixed[:, pl.ds(2 * D + first, LANES)],
            (((0,), (0,)), ((), ())),
            preferred_element_type=jnp.float32,
        )
        product = jnp.where(same, product, 0.0)
        packed = product[:HEAD_DIM]
        for h in range(1, PACK):
            packed = packed + product[h * HEAD_DIM : (h + 1) * HEAD_DIM]
        part[pl.ds(pl.multiple_of(g * HEAD_DIM, HEAD_DIM), HEAD_DIM), :] = packed
        return 0

    lax.fori_loop(0, GROUPS, outer, 0)

    def piece(ref, k):
        return ref.at[pl.ds(pl.multiple_of(k * per, 8), per)]

    def scatter(k):
        peer = lax.rem(me + k, n)
        return pltpu.make_async_remote_copy(
            src_ref=piece(part, peer),
            dst_ref=landed.at[k],
            send_sem=send1.at[k],
            recv_sem=recv1.at[k],
            device_id={"tile": peer},
            device_id_type=MESH,
        )

    def share(k):
        return pltpu.make_async_remote_copy(
            src_ref=mine,
            dst_ref=piece(state, me),
            send_sem=send2.at[k],
            recv_sem=recv2.at[k],
            device_id={"tile": lax.rem(me + k, n)},
            device_id_type=MESH,
        )

    def lay_table():
        for i in range(3):
            for j in range(3):
                flat_ref[3 * i + j : 3 * i + j + 1, :] = conv_ref[i, j : j + 1, :].astype(jnp.float32)
        flat_ref[9:10, :] = conv_bias_ref[...].astype(jnp.float32).reshape(1, 2 * FF)
        flat_ref[10:11, :] = 0.5 * in_bias_ref[...].astype(jnp.float32).reshape(1, 2 * FF)
        flat_ref[11:, :] = jnp.zeros((5, 2 * FF), jnp.float32)

        def lay(q, _):
            first = pl.multiple_of(q * LANES, LANES)
            second = pl.multiple_of(q * LANES + FF - SPLIT, LANES)
            a = flat_ref[:, pl.ds(first, LANES)]
            b = flat_ref[:, pl.ds(second, 2 * LANES)][:, SPLIT : SPLIT + LANES]
            table_ref[q] = jnp.concatenate([a, b], axis=1)
            return 0

        lax.fori_loop(0, STEPS - 1, lay, 0)
        q = STEPS - 1
        none = jnp.zeros((16, LANES - SPLIT), jnp.float32)
        a, b = flat_ref[:, q * LANES : FF], flat_ref[:, FF + q * LANES : 2 * FF]
        table_ref[q] = jnp.concatenate([a, none, b, none], axis=1)

    def each(do):
        def body(k, _):
            do(k)
            return 0

        lax.fori_loop(1, n, body, 0)

    each(lambda k: scatter(k).start())
    lay_table()
    tick(4)
    mine[...] = part[pl.ds(pl.multiple_of(me * per, 8), per), :]

    def gather(k):
        scatter(k).wait_recv()
        mine[...] += landed[k]

    each(gather)
    each(lambda k: share(k).start())
    state[pl.ds(pl.multiple_of(me * per, 8), per), :] = mine[...]
    tick(5)
    each(lambda k: scatter(k).wait_send())
    each(lambda k: share(k).wait())

    pieces = []
    for g in range(GROUPS):
        block = jnp.concatenate([state[g * HEAD_DIM : (g + 1) * HEAD_DIM, :]] * PACK, axis=0)
        block = jnp.where(same, block, 0.0)
        pieces.append(
            jnp.dot(
                mixed[:, g * LANES : (g + 1) * LANES].astype(jnp.float32),
                block,
                precision=lax.Precision.HIGHEST,
                preferred_element_type=jnp.float32,
            )
        )
    attended = jnp.concatenate(pieces, axis=1)
    gain = gain_ref[...].astype(jnp.float32).reshape(1, D)
    factor = lax.rsqrt(jnp.mean(attended * attended, axis=-1, keepdims=True) + 1e-06)
    normed[...] = (attended * factor * gain).astype(jnp.bfloat16)
    tick(6)
    loads[3].wait()

    def attach(j, _):
        cols = pl.ds(pl.multiple_of(j * span, LANES), span)
        out = jnp.dot(normed[...], proj_ref[:, cols], preferred_element_type=jnp.float32)
        after_ref[:, cols] += mod_ref[2:3, cols] * out
        return 0

    lax.fori_loop(0, 3, attach, 0)
    rounded = modulated_norm(after_ref[...], mod_ref[3:4, :], mod_ref[4:5, :]).astype(jnp.bfloat16)
    frame_ref[CANVAS_W : CANVAS_W + tokens, :] = rounded * jnp.bfloat16(0.5)

    def halo(way):
        lo = tokens if way == 0 else CANVAS_W
        to = 0 if way == 0 else CANVAS_W + tokens
        return pltpu.make_async_remote_copy(
            src_ref=frame_ref.at[lo : lo + CANVAS_W],
            dst_ref=frame_ref.at[to : to + CANVAS_W],
            send_sem=halo_send.at[way],
            recv_sem=halo_recv.at[way],
            device_id={"tile": me + (1 if way == 0 else -1)},
            device_id_type=MESH,
        )

    has = (me < n - 1, me > 0)
    for way in range(2):
        @pl.when(has[way])
        def _():
            halo(way).start()

    @pl.when(me == 0)
    def _():
        frame_ref[:CANVAS_W, :] = jnp.zeros((CANVAS_W, D), jnp.bfloat16)

    @pl.when(me == n - 1)
    def _():
        frame_ref[CANVAS_W + tokens :, :] = jnp.zeros((CANVAS_W, D), jnp.bfloat16)

    tick(7)
    for way in range(2):
        @pl.when(has[way])
        def _():
            halo(way).wait_send()

        @pl.when(has[1 - way])
        def _():
            halo(way).wait_recv()

    frame = frame_ref.shape[0]
    edge = [jnp.where(has[1 - way], 1.0, 0.0).astype(jnp.float32) for way in range(2)]
    column = lax.broadcasted_iota(jnp.int32, (8, PAIR), 0)
    not_left = column > 0
    not_right = column < 7
    acc_ref[...] = jnp.zeros_like(acc_ref)

    def gather_rows(q, i):
        for lo, hi, to in ((0, PAIR, i * PAIR), (PAIR, PAIR + LANES, 2 * PAIR + i * LANES)):
            for j in range(lo, hi, hi - lo if rows % 8 == 0 else LANES):
                for t in range(n):
                    a, b, c = t // (2 * count_b), t // 2 % count_b, t % 2
                    at = slice(t * rows, (t + 1) * rows)
                    if rows % 8 == 0:
                        wide[at, to : to + hi - lo] = land[q, a, b, c, :, lo:hi]
                    else:
                        wide32[at, :] = land[q, a, b, c, :, j : j + LANES].astype(jnp.float32)
                if rows % 8:
                    wide[:, to + j - lo : to + j - lo + LANES] = wide32[...].astype(jnp.bfloat16)

    def expand(i):
        cols = slice(i * PAIR, (i + 1) * PAIR)
        return jnp.dot(frame_ref[...], wide[:, cols], preferred_element_type=jnp.float32)

    def filtered(q, half):
        p = table_ref[q]
        half = half + p[10:11, :]
        e = (half + half * jnp.tanh(half)).astype(jnp.bfloat16).astype(jnp.float32)
        lines = [e[r * CANVAS_W : (r + 1) * CANVAS_W] for r in range(frame // CANVAS_W)]
        lines[0] = lines[0] * edge[0]
        lines[-1] = lines[-1] * edge[1]
        out = []
        for r in range(tokens // CANVAS_W):
            way = []
            for j in range(3):
                way.append(
                    lines[r] * p[j : j + 1, :]
                    + lines[r + 1] * p[3 + j : 4 + j, :]
                    + lines[r + 2] * p[6 + j : 7 + j, :]
                )
            left = pltpu.roll(way[0], 1, 0)
            left = jnp.concatenate([jnp.where(not_left, left[:8], 0.0), left[8:]], axis=0)
            right = pltpu.roll(way[2], CANVAS_W - 1, 0)
            right = jnp.concatenate([right[:-8], jnp.where(not_right, right[-8:], 0.0)], axis=0)
            conv = left + way[1] + right + p[9:10, :]
            out.append((conv[:, :LANES] * silu(conv[:, LANES:])).astype(jnp.bfloat16))
        return jnp.concatenate(out, axis=0)

    def use(g):
        w = width(g) if isinstance(g, int) else 2
        twin_in(g).wait_recv()
        for i in range(w):
            gather_rows(2 * g + i, i)
        halves = [expand(i) for i in range(w)]
        units = jnp.concatenate([filtered(2 * g + i, halves[i]) for i in range(w)], axis=1)
        acc_ref[...] += lax.dot_general(
            units,
            wide[:, 2 * PAIR : 2 * PAIR + w * LANES],
            (((1,), (1,)), ((), ())),
            preferred_element_type=jnp.float32,
        )

    double = 0
    while 2 * double + 1 <= EARLY + double - LAG_USE:
        double += 1
    shift = EARLY - double

    def catch_up(i, _):
        slot(EARLY + i)
        use(2 * i)
        use(2 * i + 1)
        return 0

    def follow(g, _):
        slot(g + shift)
        use(g)
        return 0

    lax.fori_loop(0, double, catch_up, 0)
    lax.fori_loop(2 * double, TEAMS - 1, follow, 0)
    slot(TEAMS - 1 + shift)
    use(TEAMS - 1)
    out_ref[...] = (after_ref[...] + mod_ref[5:6, :] * acc_ref[...]).astype(out_ref.dtype)
    settle()


def local(
    n,
    hidden,
    keep_mask,
    kept_embed,
    time_mod,
    timestep,
    qkv_weight,
    proj_weight,
    norm_gain,
    in_weight,
    in_bias,
    conv_weight,
    conv_bias,
    out_weight,
):
    count_a, count_b = mesh_box(n)
    rows = in_weight.shape[0]
    tokens = hidden.shape[0]
    per = -(-GROUPS * HEAD_DIM // (8 * n)) * 8
    vmem = pl.BlockSpec(memory_space=pltpu.VMEM)
    smem = pl.BlockSpec(memory_space=pltpu.SMEM)
    hbm = pl.BlockSpec(memory_space=pl.ANY)
    dma = pltpu.SemaphoreType.DMA
    bf16 = jnp.bfloat16
    f32 = jnp.float32
    return pl.pallas_call(
        functools.partial(kernel, n),
        out_shape=jax.ShapeDtypeStruct((tokens, D), bf16),
        in_specs=[smem] + [vmem] * 4 + [hbm] * 2 + [vmem] * 6,
        out_specs=vmem,
        scratch_shapes=[
            pltpu.VMEM((2, D, D), bf16),
            pltpu.VMEM((D, D), bf16),
            pltpu.VMEM((tokens, D), f32),
            pltpu.VMEM((tokens + 2 * CANVAS_W, D), bf16),
            pltpu.VMEM((tokens, 3 * D), bf16),
            pltpu.VMEM((n * per, LANES), f32),
            pltpu.VMEM((n, per, LANES), f32),
            pltpu.VMEM((per, LANES), f32),
            pltpu.VMEM((n * per, LANES), f32),
            pltpu.VMEM((tokens, D), f32),
            pltpu.VMEM((D if rows % 8 else 8, LANES), f32),
            pltpu.VMEM((16, 2 * FF), f32),
            pltpu.VMEM((STEPS, 16, PAIR), f32),
            pltpu.VMEM((8, D), f32),
            pltpu.VMEM((STEPS, count_a, count_b, 2, rows, 3 * LANES), bf16),
            dma((n,)),
            dma((n,)),
            dma((n,)),
            dma((n,)),
            dma((2,)),
            dma((2,)),
            dma((count_a,)),
            dma((TEAMS,)),
            dma((2, count_b)),
            dma((TEAMS,)),
            dma((count_a,)),
            dma,
            dma,
            dma((TEAMS,)),
            dma((4,)),
            dma,
        ],
        compiler_params=pltpu.CompilerParams(
            collective_id=0,
            has_side_effects=True,
            vmem_limit_bytes=61 << 20,
        ),
    )(
        timestep,
        hidden,
        keep_mask,
        kept_embed,
        time_mod.transpose(1, 0, 2),
        qkv_weight,
        proj_weight,
        norm_gain,
        in_weight,
        in_bias,
        conv_weight,
        conv_bias,
        out_weight.T,
    )


def solution(mesh):
    in_specs = (
        P(("groups", "tile"), None),
        P(("groups", "tile")),
        P(),
        P(),
        P("groups"),
        P(),
        P(),
        P(),
        P("tile", None),
        P(),
        P(),
        P(),
        P(None, "tile"),
    )
    return jax.shard_map(
        functools.partial(local, mesh.shape["tile"]),
        mesh=mesh,
        in_specs=in_specs,
        out_specs=P(("groups", "tile"), None),
        check_vma=False,
    )
```

```python
import functools

import jax
import jax.numpy as jnp
from jax import lax
from jax.experimental import pallas as pl
from jax.experimental.pallas import tpu as pltpu
from jax.sharding import PartitionSpec as P

D = 1152
HEADS = 36
HEAD_DIM = 32
FF = 2880
CANVAS_W = 128
LANES = 128
PACK = LANES // HEAD_DIM
GROUPS = D // LANES
MESH = pl.DeviceIdType.MESH


def mesh_box(n):
    wide = 1
    while (2 * wide) ** 2 <= n // 2:
        wide *= 2
    return n // (2 * wide), wide


STEPS = -(-FF // LANES)
SPLIT = FF % LANES
PAIR = 2 * LANES
WIDE = 1
TEAMS = -(-STEPS // WIDE)
AHEAD = 2
LAG_SIDE = 3
LAG_PLANE = 6
LAG_USE = 7
SITES = (1,2,3,4,4,5,5,6,7,7,)
EARLY = len(SITES)


def width(g):
    return min(WIDE, STEPS - WIDE * g)


def repeat(lo, hi, do):
    if hi - lo <= 4:
        for k in range(lo, hi):
            do(k)
        return

    def body(k, _):
        do(k)
        return 0

    lax.fori_loop(lo, hi, body, 0)


def modulated_norm(stream, shift, scale):
    factor = lax.rsqrt(jnp.mean(stream * stream, axis=-1, keepdims=True) + 1e-06)
    return stream * factor * (1.0 + scale) + shift


def silu(v):
    half = 0.5 * v
    return half * (1.0 + jnp.tanh(half))


def kernel(
    n,
    step_ref,
    hidden_ref,
    mask_ref,
    embed_ref,
    time_ref,
    qkv_hbm,
    proj_hbm,
    gain_ref,
    in_ref,
    in_bias_ref,
    conv_ref,
    conv_bias_ref,
    outw_ref,
    out_ref,
    qkv_ref,
    proj_ref,
    after_ref,
    frame_ref,
    mixed,
    part,
    landed,
    mine,
    state,
    acc_ref,
    wide32,
    flat_ref,
    table_ref,
    mod_ref,
    land,
    send1,
    recv1,
    send2,
    recv2,
    halo_send,
    halo_recv,
    line_send,
    line_recv,
    side_send,
    side_recv,
    far_send,
    plane_send,
    twin_send,
    twin_recv,
    load_sem,
    own_sem,
):
    count_a, count_b = mesh_box(n)
    me = lax.axis_index("tile")
    plane = lax.axis_index("groups")
    core = lax.rem(me, 2)
    at_b = lax.rem(me // 2, count_b)
    at_a = me // (2 * count_b)
    rows = in_ref.shape[0]
    per = mine.shape[0]
    tokens = hidden_ref.shape[0]
    normed = frame_ref.at[CANVAS_W : CANVAS_W + tokens]
    wide = qkv_ref.at[0, :, : 6 * LANES]

    def tile_of(a, b, c):
        return (a * count_b + b) * 2 + c

    loads = [
        pltpu.make_async_copy(
            qkv_hbm.at[:, j * D : (j + 1) * D], qkv_ref.at[j % 2], load_sem.at[j]
        )
        for j in range(3)
    ]
    loads.append(pltpu.make_async_copy(proj_hbm, proj_ref, load_sem.at[3]))
    for j in (0, 1, 3):
        loads[j].start()

    barrier = pltpu.get_barrier_semaphore()

    def greet(k, _):
        pl.semaphore_signal(
            barrier, inc=1, device_id={"tile": lax.rem(me + k, n)}, device_id_type=MESH
        )
        return 0

    lax.fori_loop(1, n, greet, 0)
    pl.semaphore_signal(barrier, inc=1, device_id={"groups": 1 - plane}, device_id_type=MESH)
    pl.semaphore_wait(barrier, n)

    def remote(ref, send, recv, target):
        return pltpu.make_async_remote_copy(
            src_ref=ref,
            dst_ref=ref,
            send_sem=send,
            recv_sem=recv,
            device_id=target,
            device_id_type=MESH,
        )

    def active(q):
        return lax.rem(plane + q, 2) == 0

    def other(k):
        return lax.rem(at_a + k, count_a)

    def beside(k):
        return lax.rem(at_b + k, count_b)

    def near(a):
        return jnp.abs(a - at_a) == 1

    def span_of(g):
        return pl.ds(WIDE * g, width(g) if isinstance(g, int) else WIDE)

    def line(g, a):
        ref = land.at[span_of(g), at_a, at_b, core]
        to = {"tile": tile_of(a, at_b, core)}
        return remote(ref, line_send.at[a], line_recv.at[g], to)

    def side(g, b, whole):
        if whole:
            ref = land.at[span_of(g), :, at_b, core]
        else:
            ref = land.at[span_of(g), at_a, at_b, core]
        to = {"tile": tile_of(at_a, b, core)}
        return remote(ref, side_send.at[int(whole), b], side_recv.at[g], to)

    def far(g, a):
        ref = land.at[span_of(g), a, at_b, core]
        return remote(ref, far_send.at[a], line_recv.at[g], {"groups": 1 - plane})

    def across(g, a, b):
        ref = land.at[span_of(g), a, b, core]
        return remote(ref, plane_send, side_recv.at[g], {"groups": 1 - plane})

    def twin(g):
        ref = land.at[span_of(g), :, :, core]
        to = {"tile": tile_of(at_a, at_b, 1 - core)}
        return remote(ref, twin_send, twin_recv.at[g], to)

    def twin_in(g):
        ref = land.at[span_of(g), :, :, 1 - core]
        to = {"tile": tile_of(at_a, at_b, 1 - core)}
        return remote(ref, own_sem, twin_recv.at[g], to)

    def own_side_in(g):
        ref = land.at[span_of(g), pl.ds(0, count_a - 1), at_b, core]
        return remote(ref, own_sem, line_recv.at[g], {"groups": 1 - plane})

    def other_side_in(g):
        ref = land.at[span_of(g), :, pl.ds(0, count_b - 1), core]
        return remote(ref, own_sem, side_recv.at[g], {"groups": 1 - plane})

    def build(q):
        first = pl.multiple_of(q * LANES, LANES)
        second = pl.multiple_of(q * LANES + FF - SPLIT, LANES)
        a = in_ref[:, pl.ds(first, LANES)]
        b = in_ref[:, pl.ds(second, 2 * LANES)][:, SPLIT : SPLIT + LANES]
        o = outw_ref[:, pl.ds(first, LANES)]
        land[q, at_a, at_b, core] = jnp.concatenate([a, b, o], axis=1)

    def build_last():
        q = STEPS - 1
        none = jnp.zeros((rows, LANES - SPLIT), jnp.bfloat16)
        a = in_ref[:, q * LANES : FF]
        b = in_ref[:, FF + q * LANES : 2 * FF]
        o = outw_ref[:, q * LANES : FF]
        land[q, at_a, at_b, core] = jnp.concatenate([a, none, b, none, o, none], axis=1)

    def gated(g, do):
        if isinstance(g, int):
            if 0 <= g < TEAMS:
                do(g)
        else:
            pl.when(jnp.logical_and(g >= 0, g < TEAMS - 1))(lambda: do(g))
            pl.when(g == TEAMS - 1)(lambda: do(TEAMS - 1))

    def start_own(g):
        if isinstance(g, int):
            for q in range(WIDE * g, WIDE * g + width(g)):
                build(q) if q < STEPS - 1 else build_last()
        else:
            for i in range(WIDE):
                build(WIDE * g + i)

        def one(k):
            a = other(k)

            @pl.when(jnp.logical_or(near(a), active(g)))
            def _():
                line(g, a).start()

        repeat(1, count_a, one)

        @pl.when(jnp.logical_not(active(g)))
        def _():
            repeat(1, count_b, lambda k: side(g, beside(k), False).start())

    def pass_lines(g):
        @pl.when(active(g))
        def _():
            own_side_in(g).wait_recv()
            repeat(1, count_b, lambda k: side(g, beside(k), True).start())

            def one(k):
                a = other(k)

                @pl.when(jnp.logical_not(near(a)))
                def _():
                    far(g, a).start()

            repeat(1, count_a, one)

    def pass_sides(g):
        @pl.when(active(g))
        def _():
            other_side_in(g).wait_recv()

            def one(k):
                b = beside(k)
                repeat(1, count_a, lambda m: across(g, other(m), b).start())

            repeat(1, count_b, one)
            twin(g).start()

    def pass_planes(g):
        @pl.when(jnp.logical_not(active(g)))
        def _():
            own_side_in(g).wait_recv()
            other_side_in(g).wait_recv()
            twin(g).start()

    def sent(ref, sem):
        remote(ref, sem, line_recv.at[0], {"groups": 1 - plane}).wait_send()

    def settle():
        shares = [sum(width(g) for g in range(TEAMS) if g % 2 == p) for p in range(2)]

        def one(k):
            a = other(k)
            pl.when(near(a))(lambda: sent(land.at[:, at_a, at_b, core], line_send.at[a]))
            for p in range(2):
                @pl.when(jnp.logical_and(jnp.logical_not(near(a)), plane == p))
                def _():
                    some = land.at[pl.ds(0, shares[p]), at_a, at_b, core]
                    sent(some, line_send.at[a])
                    sent(some, far_send.at[a])

        repeat(1, count_a, one)
        for p in range(2):
            @pl.when(plane == p)
            def _():
                on, off = pl.ds(0, shares[p]), pl.ds(0, shares[1 - p])

                def two(k):
                    b = beside(k)
                    sent(land.at[on, :, at_b, core], side_send.at[1, b])
                    sent(land.at[off, at_a, at_b, core], side_send.at[0, b])

                repeat(1, count_b, two)
                most = pl.ds(0, count_a - 1)
                sent(land.at[on, most, pl.ds(0, count_b - 1), core], plane_send)

        sent(land.at[:, :, :, core], twin_send)

    def slot(s):
        gated(s + AHEAD, start_own)
        gated(s, pass_lines)
        gated(s - LAG_SIDE, pass_sides)
        gated(s - LAG_PLANE, pass_planes)

    def tick(site):
        for s, where in enumerate(SITES):
            if where == site:
                slot(s)

    for g in range(AHEAD):
        start_own(g)

    step_at = lax.broadcasted_iota(jnp.int32, time_ref.shape[1:], 0) == step_ref[0]
    for j in range(6):
        picked = jnp.where(step_at, time_ref[j].astype(jnp.float32), 0.0)
        mod_ref[j : j + 1, :] = jnp.sum(picked, axis=0, keepdims=True)
    mask = mask_ref[...].astype(jnp.float32).reshape(tokens, 1)
    embed = embed_ref[...].astype(jnp.float32).reshape(1, D)
    stream = hidden_ref[...].astype(jnp.float32) + mask * embed
    normed[...] = modulated_norm(stream, mod_ref[0:1, :], mod_ref[1:2, :]).astype(jnp.bfloat16)
    after_ref[...] = stream
    span = D // 3

    def project(third):
        def body(i, _):
            cols = pl.ds(pl.multiple_of(i * span, LANES), span)
            out = jnp.dot(
                normed[...], qkv_ref[third % 2, :, cols], preferred_element_type=jnp.float32
            )
            if third < 2:
                out = jnp.maximum(out, 0.0)
            to = pl.ds(pl.multiple_of(third * D + i * span, LANES), span)
            mixed[:, to] = out.astype(jnp.bfloat16)
            return 0

        loads[third].wait()
        lax.fori_loop(0, 3, body, 0)
        if third == 0:
            loads[2].start()
        tick(1 + third)

    tick(0)
    for third in range(3):
        project(third)
    row_head = lax.broadcasted_iota(jnp.int32, (LANES, LANES), 0) // HEAD_DIM
    col_head = lax.broadcasted_iota(jnp.int32, (LANES, LANES), 1) // HEAD_DIM
    same = row_head == col_head
    part[...] = jnp.zeros_like(part)

    def outer(g, _):
        first = pl.multiple_of(g * LANES, LANES)
        product = lax.dot_general(
            mixed[:, pl.ds(D + first, LANES)],
            mixed[:, pl.ds(2 * D + first, LANES)],
            (((0,), (0,)), ((), ())),
            preferred_element_type=jnp.float32,
        )
        product = jnp.where(same, product, 0.0)
        packed = product[:HEAD_DIM]
        for h in range(1, PACK):
            packed = packed + product[h * HEAD_DIM : (h + 1) * HEAD_DIM]
        part[pl.ds(pl.multiple_of(g * HEAD_DIM, HEAD_DIM), HEAD_DIM), :] = packed
        return 0

    lax.fori_loop(0, GROUPS, outer, 0)

    def piece(ref, k):
        return ref.at[pl.ds(pl.multiple_of(k * per, 8), per)]

    def scatter(k):
        peer = lax.rem(me + k, n)
        return pltpu.make_async_remote_copy(
            src_ref=piece(part, peer),
            dst_ref=landed.at[k],
            send_sem=send1.at[k],
            recv_sem=recv1.at[k],
            device_id={"tile": peer},
            device_id_type=MESH,
        )

    def share(k):
        return pltpu.make_async_remote_copy(
            src_ref=mine,
            dst_ref=piece(state, me),
            send_sem=send2.at[k],
            recv_sem=recv2.at[k],
            device_id={"tile": lax.rem(me + k, n)},
            device_id_type=MESH,
        )

    def lay_table():
        for i in range(3):
            for j in range(3):
                flat_ref[3 * i + j : 3 * i + j + 1, :] = conv_ref[i, j : j + 1, :].astype(jnp.float32)
        flat_ref[9:10, :] = conv_bias_ref[...].astype(jnp.float32).reshape(1, 2 * FF)
        flat_ref[10:11, :] = 0.5 * in_bias_ref[...].astype(jnp.float32).reshape(1, 2 * FF)
        flat_ref[11:, :] = jnp.zeros((5, 2 * FF), jnp.float32)

        def lay(q, _):
            first = pl.multiple_of(q * LANES, LANES)
            second = pl.multiple_of(q * LANES + FF - SPLIT, LANES)
            a = flat_ref[:, pl.ds(first, LANES)]
            b = flat_ref[:, pl.ds(second, 2 * LANES)][:, SPLIT : SPLIT + LANES]
            table_ref[q] = jnp.concatenate([a, b], axis=1)
            return 0

        lax.fori_loop(0, STEPS - 1, lay, 0)
        q = STEPS - 1
        none = jnp.zeros((16, LANES - SPLIT), jnp.float32)
        a, b = flat_ref[:, q * LANES : FF], flat_ref[:, FF + q * LANES : 2 * FF]
        table_ref[q] = jnp.concatenate([a, none, b, none], axis=1)

    def each(do):
        def body(k, _):
            do(k)
            return 0

        lax.fori_loop(1, n, body, 0)

    each(lambda k: scatter(k).start())
    lay_table()
    tick(4)
    mine[...] = part[pl.ds(pl.multiple_of(me * per, 8), per), :]

    def gather(k):
        scatter(k).wait_recv()
        mine[...] += landed[k]

    each(gather)
    each(lambda k: share(k).start())
    state[pl.ds(pl.multiple_of(me * per, 8), per), :] = mine[...]
    tick(5)
    each(lambda k: scatter(k).wait_send())
    each(lambda k: share(k).wait())

    pieces = []
    for g in range(GROUPS):
        block = jnp.concatenate([state[g * HEAD_DIM : (g + 1) * HEAD_DIM, :]] * PACK, axis=0)
        block = jnp.where(same, block, 0.0)
        query = mixed[:, g * LANES : (g + 1) * LANES]
        total = None
        for _ in range(3):
            term = block.astype(jnp.bfloat16)
            block = block - term.astype(jnp.float32)
            out = jnp.dot(query, term, preferred_element_type=jnp.float32)
            total = out if total is None else total + out
        pieces.append(total)
    attended = jnp.concatenate(pieces, axis=1)
    gain = gain_ref[...].astype(jnp.float32).reshape(1, D)
    factor = lax.rsqrt(jnp.mean(attended * attended, axis=-1, keepdims=True) + 1e-06)
    normed[...] = (attended * factor * gain).astype(jnp.bfloat16)
    tick(6)
    loads[3].wait()

    def attach(j, _):
        cols = pl.ds(pl.multiple_of(j * span, LANES), span)
        out = jnp.dot(normed[...], proj_ref[:, cols], preferred_element_type=jnp.float32)
        after_ref[:, cols] += mod_ref[2:3, cols] * out
        return 0

    lax.fori_loop(0, 3, attach, 0)
    rounded = modulated_norm(after_ref[...], mod_ref[3:4, :], mod_ref[4:5, :]).astype(jnp.bfloat16)
    frame_ref[CANVAS_W : CANVAS_W + tokens, :] = rounded * jnp.bfloat16(0.5)

    def halo(way):
        lo = tokens if way == 0 else CANVAS_W
        to = 0 if way == 0 else CANVAS_W + tokens
        return pltpu.make_async_remote_copy(
            src_ref=frame_ref.at[lo : lo + CANVAS_W],
            dst_ref=frame_ref.at[to : to + CANVAS_W],
            send_sem=halo_send.at[way],
            recv_sem=halo_recv.at[way],
            device_id={"tile": me + (1 if way == 0 else -1)},
            device_id_type=MESH,
        )

    has = (me < n - 1, me > 0)
    for way in range(2):
        @pl.when(has[way])
        def _():
            halo(way).start()

    @pl.when(me == 0)
    def _():
        frame_ref[:CANVAS_W, :] = jnp.zeros((CANVAS_W, D), jnp.bfloat16)

    @pl.when(me == n - 1)
    def _():
        frame_ref[CANVAS_W + tokens :, :] = jnp.zeros((CANVAS_W, D), jnp.bfloat16)

    tick(7)
    for way in range(2):
        @pl.when(has[way])
        def _():
            halo(way).wait_send()

        @pl.when(has[1 - way])
        def _():
            halo(way).wait_recv()

    frame = frame_ref.shape[0]
    edge = [jnp.where(has[1 - way], 1.0, 0.0).astype(jnp.float32) for way in range(2)]
    column = lax.broadcasted_iota(jnp.int32, (8, PAIR), 0)
    not_left = column > 0
    not_right = column < 7
    acc_ref[...] = jnp.zeros_like(acc_ref)

    def gather_rows(q, i):
        for lo, hi, to in ((0, PAIR, i * PAIR), (PAIR, PAIR + LANES, 2 * PAIR + i * LANES)):
            for j in range(lo, hi, hi - lo if rows % 8 == 0 else LANES):
                for t in range(n):
                    a, b, c = t // (2 * count_b), t // 2 % count_b, t % 2
                    at = slice(t * rows, (t + 1) * rows)
                    if rows % 8 == 0:
                        wide[at, to : to + hi - lo] = land[q, a, b, c, :, lo:hi]
                    else:
                        wide32[at, :] = land[q, a, b, c, :, j : j + LANES].astype(jnp.float32)
                if rows % 8:
                    wide[:, to + j - lo : to + j - lo + LANES] = wide32[...].astype(jnp.bfloat16)

    def expand(i):
        cols = slice(i * PAIR, (i + 1) * PAIR)
        return jnp.dot(frame_ref[...], wide[:, cols], preferred_element_type=jnp.float32)

    def filtered(q, half):
        p = table_ref[q]
        half = half + p[10:11, :]
        e = (half + half * jnp.tanh(half)).astype(jnp.bfloat16).astype(jnp.float32)
        lines = [e[r * CANVAS_W : (r + 1) * CANVAS_W] for r in range(frame // CANVAS_W)]
        lines[0] = lines[0] * edge[0]
        lines[-1] = lines[-1] * edge[1]
        out = []
        for r in range(tokens // CANVAS_W):
            way = []
            for j in range(3):
                way.append(
                    lines[r] * p[j : j + 1, :]
                    + lines[r + 1] * p[3 + j : 4 + j, :]
                    + lines[r + 2] * p[6 + j : 7 + j, :]
                )
            left = pltpu.roll(way[0], 1, 0)
            left = jnp.concatenate([jnp.where(not_left, left[:8], 0.0), left[8:]], axis=0)
            right = pltpu.roll(way[2], CANVAS_W - 1, 0)
            right = jnp.concatenate([right[:-8], jnp.where(not_right, right[-8:], 0.0)], axis=0)
            conv = left + way[1] + right + p[9:10, :]
            out.append((conv[:, :LANES] * silu(conv[:, LANES:])).astype(jnp.bfloat16))
        return jnp.concatenate(out, axis=0)

    def use(g):
        w = width(g) if isinstance(g, int) else WIDE
        twin_in(g).wait_recv()
        for i in range(w):
            gather_rows(WIDE * g + i, i)
        halves = [expand(i) for i in range(w)]
        units = jnp.concatenate([filtered(WIDE * g + i, halves[i]) for i in range(w)], axis=1)
        acc_ref[...] += lax.dot_general(
            units,
            wide[:, 2 * PAIR : 2 * PAIR + w * LANES],
            (((1,), (1,)), ((), ())),
            preferred_element_type=jnp.float32,
        )

    double = 0
    while 2 * double + 1 <= EARLY + double - LAG_USE:
        double += 1
    shift = EARLY - double

    def catch_up(i, _):
        slot(EARLY + i)
        use(2 * i)
        use(2 * i + 1)
        return 0

    def follow(g, _):
        slot(g + shift)
        use(g)
        return 0

    lax.fori_loop(0, double, catch_up, 0)
    lax.fori_loop(2 * double, TEAMS - 1, follow, 0)
    slot(TEAMS - 1 + shift)
    use(TEAMS - 1)
    out_ref[...] = (after_ref[...] + mod_ref[5:6, :] * acc_ref[...]).astype(out_ref.dtype)
    settle()


def local(
    n,
    hidden,
    keep_mask,
    kept_embed,
    time_mod,
    timestep,
    qkv_weight,
    proj_weight,
    norm_gain,
    in_weight,
    in_bias,
    conv_weight,
    conv_bias,
    out_weight,
):
    count_a, count_b = mesh_box(n)
    rows = in_weight.shape[0]
    tokens = hidden.shape[0]
    per = -(-GROUPS * HEAD_DIM // (8 * n)) * 8
    vmem = pl.BlockSpec(memory_space=pltpu.VMEM)
    smem = pl.BlockSpec(memory_space=pltpu.SMEM)
    hbm = pl.BlockSpec(memory_space=pl.ANY)
    dma = pltpu.SemaphoreType.DMA
    bf16 = jnp.bfloat16
    f32 = jnp.float32
    return pl.pallas_call(
        functools.partial(kernel, n),
        out_shape=jax.ShapeDtypeStruct((tokens, D), bf16),
        in_specs=[smem] + [vmem] * 4 + [hbm] * 2 + [vmem] * 6,
        out_specs=vmem,
        scratch_shapes=[
            pltpu.VMEM((2, D, D), bf16),
            pltpu.VMEM((D, D), bf16),
            pltpu.VMEM((tokens, D), f32),
            pltpu.VMEM((tokens + 2 * CANVAS_W, D), bf16),
            pltpu.VMEM((tokens, 3 * D), bf16),
            pltpu.VMEM((n * per, LANES), f32),
            pltpu.VMEM((n, per, LANES), f32),
            pltpu.VMEM((per, LANES), f32),
            pltpu.VMEM((n * per, LANES), f32),
            pltpu.VMEM((tokens, D), f32),
            pltpu.VMEM((D if rows % 8 else 8, LANES), f32),
            pltpu.VMEM((16, 2 * FF), f32),
            pltpu.VMEM((STEPS, 16, PAIR), f32),
            pltpu.VMEM((8, D), f32),
            pltpu.VMEM((STEPS, count_a, count_b, 2, rows, 3 * LANES), bf16),
            dma((n,)),
            dma((n,)),
            dma((n,)),
            dma((n,)),
            dma((2,)),
            dma((2,)),
            dma((count_a,)),
            dma((TEAMS,)),
            dma((2, count_b)),
            dma((TEAMS,)),
            dma((count_a,)),
            dma,
            dma,
            dma((TEAMS,)),
            dma((4,)),
            dma,
        ],
        compiler_params=pltpu.CompilerParams(
            collective_id=0,
            has_side_effects=True,
            vmem_limit_bytes=61 << 20,
        ),
    )(
        timestep,
        hidden,
        keep_mask,
        kept_embed,
        time_mod.transpose(1, 0, 2),
        qkv_weight,
        proj_weight,
        norm_gain,
        in_weight,
        in_bias,
        conv_weight,
        conv_bias,
        out_weight.T,
    )


def solution(mesh):
    in_specs = (
        P(("groups", "tile"), None),
        P(("groups", "tile")),
        P(),
        P(),
        P("groups"),
        P(),
        P(),
        P(),
        P("tile", None),
        P(),
        P(),
        P(),
        P(None, "tile"),
    )
    return jax.shard_map(
        functools.partial(local, mesh.shape["tile"]),
        mesh=mesh,
        in_specs=in_specs,
        out_specs=P(("groups", "tile"), None),
        check_vma=False,
    )
```

```python
import functools

import jax
import jax.numpy as jnp
from jax import lax
from jax.experimental import pallas as pl
from jax.experimental.pallas import tpu as pltpu
from jax.sharding import PartitionSpec as P

D = 1152
HEADS = 36
HEAD_DIM = 32
FF = 2880
CANVAS_W = 128
LANES = 128
PACK = LANES // HEAD_DIM
GROUPS = D // LANES
MESH = pl.DeviceIdType.MESH


def mesh_box(n):
    wide = 1
    while (2 * wide) ** 2 <= n // 2:
        wide *= 2
    return n // (2 * wide), wide


STEPS = -(-FF // LANES)
SPLIT = FF % LANES
PAIR = 2 * LANES
WIDE = 1
TEAMS = -(-STEPS // WIDE)
AHEAD = 2
LAG_SIDE = 3
LAG_PLANE = 6
LAG_USE = 7
SITES = (1,2,3,4,4,5,5,6,7,7,)
EARLY = len(SITES)


def width(g):
    return min(WIDE, STEPS - WIDE * g)


def repeat(lo, hi, do):
    if hi - lo <= 4:
        for k in range(lo, hi):
            do(k)
        return

    def body(k, _):
        do(k)
        return 0

    lax.fori_loop(lo, hi, body, 0)


def modulated_norm(stream, shift, scale):
    factor = lax.rsqrt(jnp.mean(stream * stream, axis=-1, keepdims=True) + 1e-06)
    return stream * factor * (1.0 + scale) + shift


def silu(v):
    half = 0.5 * v
    return half * (1.0 + jnp.tanh(half))


def kernel(
    n,
    step_ref,
    hidden_ref,
    mask_ref,
    embed_ref,
    time_ref,
    qkv_hbm,
    proj_hbm,
    gain_ref,
    in_ref,
    in_bias_ref,
    conv_ref,
    conv_bias_ref,
    outw_ref,
    out_ref,
    qkv_ref,
    proj_ref,
    after_ref,
    frame_ref,
    mixed,
    part,
    landed,
    mine,
    state,
    acc_ref,
    wide32,
    flat_ref,
    table_ref,
    mod_ref,
    land,
    send1,
    recv1,
    send2,
    recv2,
    halo_send,
    halo_recv,
    line_send,
    line_recv,
    side_send,
    side_recv,
    far_send,
    plane_send,
    twin_send,
    twin_recv,
    load_sem,
    own_sem,
):
    count_a, count_b = mesh_box(n)
    me = lax.axis_index("tile")
    plane = lax.axis_index("groups")
    core = lax.rem(me, 2)
    at_b = lax.rem(me // 2, count_b)
    at_a = me // (2 * count_b)
    rows = in_ref.shape[0]
    per = mine.shape[0]
    tokens = hidden_ref.shape[0]
    normed = frame_ref.at[CANVAS_W : CANVAS_W + tokens]
    wide = qkv_ref.at[0, :, : 6 * LANES]

    def tile_of(a, b, c):
        return (a * count_b + b) * 2 + c

    loads = [
        pltpu.make_async_copy(
            qkv_hbm.at[:, j * D : (j + 1) * D], qkv_ref.at[j % 2], load_sem.at[j]
        )
        for j in range(3)
    ]
    loads.append(pltpu.make_async_copy(proj_hbm, proj_ref, load_sem.at[3]))
    for j in (0, 1, 3):
        loads[j].start()

    barrier = pltpu.get_barrier_semaphore()

    def greet(k, _):
        pl.semaphore_signal(
            barrier, inc=1, device_id={"tile": lax.rem(me + k, n)}, device_id_type=MESH
        )
        return 0

    lax.fori_loop(1, n, greet, 0)
    pl.semaphore_signal(barrier, inc=1, device_id={"groups": 1 - plane}, device_id_type=MESH)
    pl.semaphore_wait(barrier, n)

    def remote(ref, send, recv, target):
        return pltpu.make_async_remote_copy(
            src_ref=ref,
            dst_ref=ref,
            send_sem=send,
            recv_sem=recv,
            device_id=target,
            device_id_type=MESH,
        )

    def active(q):
        return lax.rem(plane + q, 2) == 0

    def other(k):
        return lax.rem(at_a + k, count_a)

    def beside(k):
        return lax.rem(at_b + k, count_b)

    def near(a):
        return jnp.abs(a - at_a) == 1

    def span_of(g):
        return pl.ds(WIDE * g, width(g) if isinstance(g, int) else WIDE)

    def line(g, a):
        ref = land.at[span_of(g), at_a, at_b, core]
        to = {"tile": tile_of(a, at_b, core)}
        return remote(ref, line_send.at[a], line_recv.at[g], to)

    def side(g, b, whole):
        if whole:
            ref = land.at[span_of(g), :, at_b, core]
        else:
            ref = land.at[span_of(g), at_a, at_b, core]
        to = {"tile": tile_of(at_a, b, core)}
        return remote(ref, side_send.at[int(whole), b], side_recv.at[g], to)

    def far(g, a):
        ref = land.at[span_of(g), a, at_b, core]
        return remote(ref, far_send.at[a], line_recv.at[g], {"groups": 1 - plane})

    def across(g, a, b):
        ref = land.at[span_of(g), a, b, core]
        return remote(ref, plane_send, side_recv.at[g], {"groups": 1 - plane})

    def twin(g):
        ref = land.at[span_of(g), :, :, core]
        to = {"tile": tile_of(at_a, at_b, 1 - core)}
        return remote(ref, twin_send, twin_recv.at[g], to)

    def twin_in(g):
        ref = land.at[span_of(g), :, :, 1 - core]
        to = {"tile": tile_of(at_a, at_b, 1 - core)}
        return remote(ref, own_sem, twin_recv.at[g], to)

    def own_side_in(g):
        ref = land.at[span_of(g), pl.ds(0, count_a - 1), at_b, core]
        return remote(ref, own_sem, line_recv.at[g], {"groups": 1 - plane})

    def other_side_in(g):
        ref = land.at[span_of(g), :, pl.ds(0, count_b - 1), core]
        return remote(ref, own_sem, side_recv.at[g], {"groups": 1 - plane})

    def build(q):
        first = pl.multiple_of(q * LANES, LANES)
        second = pl.multiple_of(q * LANES + FF - SPLIT, LANES)
        a = in_ref[:, pl.ds(first, LANES)]
        b = in_ref[:, pl.ds(second, 2 * LANES)][:, SPLIT : SPLIT + LANES]
        o = outw_ref[:, pl.ds(first, LANES)]
        land[q, at_a, at_b, core] = jnp.concatenate([a, b, o], axis=1)

    def build_last():
        q = STEPS - 1
        none = jnp.zeros((rows, LANES - SPLIT), jnp.bfloat16)
        a = in_ref[:, q * LANES : FF]
        b = in_ref[:, FF + q * LANES : 2 * FF]
        o = outw_ref[:, q * LANES : FF]
        land[q, at_a, at_b, core] = jnp.concatenate([a, none, b, none, o, none], axis=1)

    def gated(g, do):
        if isinstance(g, int):
            if 0 <= g < TEAMS:
                do(g)
        else:
            pl.when(jnp.logical_and(g >= 0, g < TEAMS - 1))(lambda: do(g))
            pl.when(g == TEAMS - 1)(lambda: do(TEAMS - 1))

    def start_own(g):
        if isinstance(g, int):
            for q in range(WIDE * g, WIDE * g + width(g)):
                build(q) if q < STEPS - 1 else build_last()
        else:
            for i in range(WIDE):
                build(WIDE * g + i)

        def one(k):
            a = other(k)

            @pl.when(jnp.logical_and(jnp.logical_not(near(a)), active(g)))
            def _():
                line(g, a).start()

        def close(k):
            a = other(k)

            @pl.when(near(a))
            def _():
                line(g, a).start()

        repeat(1, count_a, one)
        repeat(1, count_a, close)

        @pl.when(jnp.logical_not(active(g)))
        def _():
            repeat(1, count_b, lambda k: side(g, beside(k), False).start())

    def pass_lines(g):
        @pl.when(active(g))
        def _():
            own_side_in(g).wait_recv()
            repeat(1, count_b, lambda k: side(g, beside(k), True).start())

            def one(k):
                a = other(k)

                @pl.when(jnp.logical_not(near(a)))
                def _():
                    far(g, a).start()

            repeat(1, count_a, one)

    def pass_sides(g):
        @pl.when(active(g))
        def _():
            other_side_in(g).wait_recv()

            def one(k):
                b = beside(k)
                repeat(1, count_a, lambda m: across(g, other(m), b).start())

            repeat(1, count_b, one)
            twin(g).start()

    def pass_planes(g):
        @pl.when(jnp.logical_not(active(g)))
        def _():
            own_side_in(g).wait_recv()
            other_side_in(g).wait_recv()
            twin(g).start()

    def sent(ref, sem):
        remote(ref, sem, line_recv.at[0], {"groups": 1 - plane}).wait_send()

    def settle():
        shares = [sum(width(g) for g in range(TEAMS) if g % 2 == p) for p in range(2)]

        def one(k):
            a = other(k)
            pl.when(near(a))(lambda: sent(land.at[:, at_a, at_b, core], line_send.at[a]))
            for p in range(2):
                @pl.when(jnp.logical_and(jnp.logical_not(near(a)), plane == p))
                def _():
                    some = land.at[pl.ds(0, shares[p]), at_a, at_b, core]
                    sent(some, line_send.at[a])
                    sent(some, far_send.at[a])

        repeat(1, count_a, one)
        for p in range(2):
            @pl.when(plane == p)
            def _():
                on, off = pl.ds(0, shares[p]), pl.ds(0, shares[1 - p])

                def two(k):
                    b = beside(k)
                    sent(land.at[on, :, at_b, core], side_send.at[1, b])
                    sent(land.at[off, at_a, at_b, core], side_send.at[0, b])

                repeat(1, count_b, two)
                most = pl.ds(0, count_a - 1)
                sent(land.at[on, most, pl.ds(0, count_b - 1), core], plane_send)

        sent(land.at[:, :, :, core], twin_send)

    def slot(s):
        gated(s + AHEAD, start_own)
        gated(s, pass_lines)
        gated(s - LAG_SIDE, pass_sides)
        gated(s - LAG_PLANE, pass_planes)

    def tick(site):
        for s, where in enumerate(SITES):
            if where == site:
                slot(s)

    for g in range(AHEAD):
        start_own(g)

    step_at = lax.broadcasted_iota(jnp.int32, time_ref.shape[1:], 0) == step_ref[0]
    for j in range(6):
        picked = jnp.where(step_at, time_ref[j].astype(jnp.float32), 0.0)
        mod_ref[j : j + 1, :] = jnp.sum(picked, axis=0, keepdims=True)
    mask = mask_ref[...].astype(jnp.float32).reshape(tokens, 1)
    embed = embed_ref[...].astype(jnp.float32).reshape(1, D)
    stream = hidden_ref[...].astype(jnp.float32) + mask * embed
    normed[...] = modulated_norm(stream, mod_ref[0:1, :], mod_ref[1:2, :]).astype(jnp.bfloat16)
    after_ref[...] = stream
    span = D // 3

    def project(third):
        def body(i, _):
            cols = pl.ds(pl.multiple_of(i * span, LANES), span)
            out = jnp.dot(
                normed[...], qkv_ref[third % 2, :, cols], preferred_element_type=jnp.float32
            )
            if third < 2:
                out = jnp.maximum(out, 0.0)
            to = pl.ds(pl.multiple_of(third * D + i * span, LANES), span)
            mixed[:, to] = out.astype(jnp.bfloat16)
            return 0

        loads[third].wait()
        lax.fori_loop(0, 3, body, 0)
        if third == 0:
            loads[2].start()
        tick(1 + third)

    tick(0)
    for third in range(3):
        project(third)
    row_head = lax.broadcasted_iota(jnp.int32, (LANES, LANES), 0) // HEAD_DIM
    col_head = lax.broadcasted_iota(jnp.int32, (LANES, LANES), 1) // HEAD_DIM
    same = row_head == col_head
    part[...] = jnp.zeros_like(part)

    def outer(g, _):
        first = pl.multiple_of(g * LANES, LANES)
        product = lax.dot_general(
            mixed[:, pl.ds(D + first, LANES)],
            mixed[:, pl.ds(2 * D + first, LANES)],
            (((0,), (0,)), ((), ())),
            preferred_element_type=jnp.float32,
        )
        product = jnp.where(same, product, 0.0)
        packed = product[:HEAD_DIM]
        for h in range(1, PACK):
            packed = packed + product[h * HEAD_DIM : (h + 1) * HEAD_DIM]
        part[pl.ds(pl.multiple_of(g * HEAD_DIM, HEAD_DIM), HEAD_DIM), :] = packed
        return 0

    lax.fori_loop(0, GROUPS, outer, 0)

    def piece(ref, k):
        return ref.at[pl.ds(pl.multiple_of(k * per, 8), per)]

    def scatter(k):
        peer = lax.rem(me + k, n)
        return pltpu.make_async_remote_copy(
            src_ref=piece(part, peer),
            dst_ref=landed.at[k],
            send_sem=send1.at[k],
            recv_sem=recv1.at[k],
            device_id={"tile": peer},
            device_id_type=MESH,
        )

    def share(k):
        return pltpu.make_async_remote_copy(
            src_ref=mine,
            dst_ref=piece(state, me),
            send_sem=send2.at[k],
            recv_sem=recv2.at[k],
            device_id={"tile": lax.rem(me + k, n)},
            device_id_type=MESH,
        )

    def lay_table():
        for i in range(3):
            for j in range(3):
                flat_ref[3 * i + j : 3 * i + j + 1, :] = conv_ref[i, j : j + 1, :].astype(jnp.float32)
        flat_ref[9:10, :] = conv_bias_ref[...].astype(jnp.float32).reshape(1, 2 * FF)
        flat_ref[10:11, :] = 0.5 * in_bias_ref[...].astype(jnp.float32).reshape(1, 2 * FF)
        flat_ref[11:, :] = jnp.zeros((5, 2 * FF), jnp.float32)

        def lay(q, _):
            first = pl.multiple_of(q * LANES, LANES)
            second = pl.multiple_of(q * LANES + FF - SPLIT, LANES)
            a = flat_ref[:, pl.ds(first, LANES)]
            b = flat_ref[:, pl.ds(second, 2 * LANES)][:, SPLIT : SPLIT + LANES]
            table_ref[q] = jnp.concatenate([a, b], axis=1)
            return 0

        lax.fori_loop(0, STEPS - 1, lay, 0)
        q = STEPS - 1
        none = jnp.zeros((16, LANES - SPLIT), jnp.float32)
        a, b = flat_ref[:, q * LANES : FF], flat_ref[:, FF + q * LANES : 2 * FF]
        table_ref[q] = jnp.concatenate([a, none, b, none], axis=1)

    def each(do):
        def body(k, _):
            do(k)
            return 0

        lax.fori_loop(1, n, body, 0)

    each(lambda k: scatter(k).start())
    lay_table()
    tick(4)
    mine[...] = part[pl.ds(pl.multiple_of(me * per, 8), per), :]

    def gather(k):
        scatter(k).wait_recv()
        mine[...] += landed[k]

    each(gather)
    each(lambda k: share(k).start())
    state[pl.ds(pl.multiple_of(me * per, 8), per), :] = mine[...]
    tick(5)
    each(lambda k: scatter(k).wait_send())
    each(lambda k: share(k).wait())

    pieces = []
    for g in range(GROUPS):
        block = jnp.concatenate([state[g * HEAD_DIM : (g + 1) * HEAD_DIM, :]] * PACK, axis=0)
        block = jnp.where(same, block, 0.0)
        query = mixed[:, g * LANES : (g + 1) * LANES]
        total = None
        for _ in range(3):
            term = block.astype(jnp.bfloat16)
            block = block - term.astype(jnp.float32)
            out = jnp.dot(query, term, preferred_element_type=jnp.float32)
            total = out if total is None else total + out
        pieces.append(total)
    attended = jnp.concatenate(pieces, axis=1)
    gain = gain_ref[...].astype(jnp.float32).reshape(1, D)
    factor = lax.rsqrt(jnp.mean(attended * attended, axis=-1, keepdims=True) + 1e-06)
    normed[...] = (attended * factor * gain).astype(jnp.bfloat16)
    tick(6)
    loads[3].wait()

    def attach(j, _):
        cols = pl.ds(pl.multiple_of(j * span, LANES), span)
        out = jnp.dot(normed[...], proj_ref[:, cols], preferred_element_type=jnp.float32)
        after_ref[:, cols] += mod_ref[2:3, cols] * out
        return 0

    lax.fori_loop(0, 3, attach, 0)
    rounded = modulated_norm(after_ref[...], mod_ref[3:4, :], mod_ref[4:5, :]).astype(jnp.bfloat16)
    frame_ref[CANVAS_W : CANVAS_W + tokens, :] = rounded * jnp.bfloat16(0.5)

    def halo(way):
        lo = tokens if way == 0 else CANVAS_W
        to = 0 if way == 0 else CANVAS_W + tokens
        return pltpu.make_async_remote_copy(
            src_ref=frame_ref.at[lo : lo + CANVAS_W],
            dst_ref=frame_ref.at[to : to + CANVAS_W],
            send_sem=halo_send.at[way],
            recv_sem=halo_recv.at[way],
            device_id={"tile": me + (1 if way == 0 else -1)},
            device_id_type=MESH,
        )

    has = (me < n - 1, me > 0)
    for way in range(2):
        @pl.when(has[way])
        def _():
            halo(way).start()

    @pl.when(me == 0)
    def _():
        frame_ref[:CANVAS_W, :] = jnp.zeros((CANVAS_W, D), jnp.bfloat16)

    @pl.when(me == n - 1)
    def _():
        frame_ref[CANVAS_W + tokens :, :] = jnp.zeros((CANVAS_W, D), jnp.bfloat16)

    tick(7)
    for way in range(2):
        @pl.when(has[way])
        def _():
            halo(way).wait_send()

        @pl.when(has[1 - way])
        def _():
            halo(way).wait_recv()

    frame = frame_ref.shape[0]
    edge = [jnp.where(has[1 - way], 1.0, 0.0).astype(jnp.float32) for way in range(2)]
    column = lax.broadcasted_iota(jnp.int32, (8, PAIR), 0)
    not_left = column > 0
    not_right = column < 7
    acc_ref[...] = jnp.zeros_like(acc_ref)

    def gather_rows(q, i):
        for lo, hi, to in ((0, PAIR, i * PAIR), (PAIR, PAIR + LANES, 2 * PAIR + i * LANES)):
            for j in range(lo, hi, hi - lo if rows % 8 == 0 else LANES):
                for t in range(n):
                    a, b, c = t // (2 * count_b), t // 2 % count_b, t % 2
                    at = slice(t * rows, (t + 1) * rows)
                    if rows % 8 == 0:
                        wide[at, to : to + hi - lo] = land[q, a, b, c, :, lo:hi]
                    else:
                        wide32[at, :] = land[q, a, b, c, :, j : j + LANES].astype(jnp.float32)
                if rows % 8:
                    wide[:, to + j - lo : to + j - lo + LANES] = wide32[...].astype(jnp.bfloat16)

    def expand(i):
        cols = slice(i * PAIR, (i + 1) * PAIR)
        return jnp.dot(frame_ref[...], wide[:, cols], preferred_element_type=jnp.float32)

    def filtered(q, half):
        p = table_ref[q]
        half = half + p[10:11, :]
        e = (half + half * jnp.tanh(half)).astype(jnp.bfloat16).astype(jnp.float32)
        lines = [e[r * CANVAS_W : (r + 1) * CANVAS_W] for r in range(frame // CANVAS_W)]
        lines[0] = lines[0] * edge[0]
        lines[-1] = lines[-1] * edge[1]
        out = []
        for r in range(tokens // CANVAS_W):
            way = []
            for j in range(3):
                way.append(
                    lines[r] * p[j : j + 1, :]
                    + lines[r + 1] * p[3 + j : 4 + j, :]
                    + lines[r + 2] * p[6 + j : 7 + j, :]
                )
            left = pltpu.roll(way[0], 1, 0)
            left = jnp.concatenate([jnp.where(not_left, left[:8], 0.0), left[8:]], axis=0)
            right = pltpu.roll(way[2], CANVAS_W - 1, 0)
            right = jnp.concatenate([right[:-8], jnp.where(not_right, right[-8:], 0.0)], axis=0)
            conv = left + way[1] + right + p[9:10, :]
            out.append((conv[:, :LANES] * silu(conv[:, LANES:])).astype(jnp.bfloat16))
        return jnp.concatenate(out, axis=0)

    def use(g):
        w = width(g) if isinstance(g, int) else WIDE
        twin_in(g).wait_recv()
        for i in range(w):
            gather_rows(WIDE * g + i, i)
        halves = [expand(i) for i in range(w)]
        units = jnp.concatenate([filtered(WIDE * g + i, halves[i]) for i in range(w)], axis=1)
        acc_ref[...] += lax.dot_general(
            units,
            wide[:, 2 * PAIR : 2 * PAIR + w * LANES],
            (((1,), (1,)), ((), ())),
            preferred_element_type=jnp.float32,
        )

    double = 0
    while 2 * double + 1 <= EARLY + double - LAG_USE:
        double += 1
    shift = EARLY - double

    def catch_up(i, _):
        slot(EARLY + i)
        use(2 * i)
        use(2 * i + 1)
        return 0

    def follow(g, _):
        slot(g + shift)
        use(g)
        return 0

    lax.fori_loop(0, double, catch_up, 0)
    lax.fori_loop(2 * double, TEAMS - 1, follow, 0)
    slot(TEAMS - 1 + shift)
    use(TEAMS - 1)
    out_ref[...] = (after_ref[...] + mod_ref[5:6, :] * acc_ref[...]).astype(out_ref.dtype)
    settle()


def local(
    n,
    hidden,
    keep_mask,
    kept_embed,
    time_mod,
    timestep,
    qkv_weight,
    proj_weight,
    norm_gain,
    in_weight,
    in_bias,
    conv_weight,
    conv_bias,
    out_weight,
):
    count_a, count_b = mesh_box(n)
    rows = in_weight.shape[0]
    tokens = hidden.shape[0]
    per = -(-GROUPS * HEAD_DIM // (8 * n)) * 8
    vmem = pl.BlockSpec(memory_space=pltpu.VMEM)
    smem = pl.BlockSpec(memory_space=pltpu.SMEM)
    hbm = pl.BlockSpec(memory_space=pl.ANY)
    dma = pltpu.SemaphoreType.DMA
    bf16 = jnp.bfloat16
    f32 = jnp.float32
    return pl.pallas_call(
        functools.partial(kernel, n),
        out_shape=jax.ShapeDtypeStruct((tokens, D), bf16),
        in_specs=[smem] + [vmem] * 4 + [hbm] * 2 + [vmem] * 6,
        out_specs=vmem,
        scratch_shapes=[
            pltpu.VMEM((2, D, D), bf16),
            pltpu.VMEM((D, D), bf16),
            pltpu.VMEM((tokens, D), f32),
            pltpu.VMEM((tokens + 2 * CANVAS_W, D), bf16),
            pltpu.VMEM((tokens, 3 * D), bf16),
            pltpu.VMEM((n * per, LANES), f32),
            pltpu.VMEM((n, per, LANES), f32),
            pltpu.VMEM((per, LANES), f32),
            pltpu.VMEM((n * per, LANES), f32),
            pltpu.VMEM((tokens, D), f32),
            pltpu.VMEM((D if rows % 8 else 8, LANES), f32),
            pltpu.VMEM((16, 2 * FF), f32),
            pltpu.VMEM((STEPS, 16, PAIR), f32),
            pltpu.VMEM((8, D), f32),
            pltpu.VMEM((STEPS, count_a, count_b, 2, rows, 3 * LANES), bf16),
            dma((n,)),
            dma((n,)),
            dma((n,)),
            dma((n,)),
            dma((2,)),
            dma((2,)),
            dma((count_a,)),
            dma((TEAMS,)),
            dma((2, count_b)),
            dma((TEAMS,)),
            dma((count_a,)),
            dma,
            dma,
            dma((TEAMS,)),
            dma((4,)),
            dma,
        ],
        compiler_params=pltpu.CompilerParams(
            collective_id=0,
            has_side_effects=True,
            vmem_limit_bytes=61 << 20,
        ),
    )(
        timestep,
        hidden,
        keep_mask,
        kept_embed,
        time_mod.transpose(1, 0, 2),
        qkv_weight,
        proj_weight,
        norm_gain,
        in_weight,
        in_bias,
        conv_weight,
        conv_bias,
        out_weight.T,
    )


def solution(mesh):
    in_specs = (
        P(("groups", "tile"), None),
        P(("groups", "tile")),
        P(),
        P(),
        P("groups"),
        P(),
        P(),
        P(),
        P("tile", None),
        P(),
        P(),
        P(),
        P(None, "tile"),
    )
    return jax.shard_map(
        functools.partial(local, mesh.shape["tile"]),
        mesh=mesh,
        in_specs=in_specs,
        out_specs=P(("groups", "tile"), None),
        check_vma=False,
    )
```
